32 devices in a mesh: seq: 4 (over z), dp: 8 (over y, x, core).
Axes of the slice: x: 2, y: 2, z: 4, core: 2. Of those that a mesh axis runs over, the one named last changes fastest.
Arguments:
- layer_input: bfloat16 [8, 2048, 768], P('dp', 'seq'), may hold values from -6 to 6
- triple_weight: bfloat16 [768, 2304], P('dp'), may hold values from -0.21875 to 0.21875
- query_bias: bfloat16 [768], P('dp'), may hold values from -3 to 3
- value_bias: bfloat16 [768], P('dp'), may hold values from -3 to 3
- mixer_weight: bfloat16 [768, 768], P('dp'), may hold values from -4 to 4
- mixer_bias: bfloat16 [768], P('dp'), may hold values from -1.75 to 1.75
- first_gain: bfloat16 [768], P('dp'), may hold values from 0.5 to 1.5
- first_shift: bfloat16 [768], P('dp'), may hold values from -1.75 to 1.75
- expand_weight: bfloat16 [768, 3072], P('dp'), may hold values from -0.21875 to 0.21875
- expand_bias: bfloat16 [3072], P('dp'), may hold values from -1.75 to 1.75
- shrink_weight: bfloat16 [3072, 768], P('dp'), may hold values from -0.109375 to 0.109375
- shrink_bias: bfloat16 [768], P('dp'), may hold values from -1.75 to 1.75
- second_gain: bfloat16 [768], P('dp'), may hold values from 0.5 to 1.5
- second_shift: bfloat16 [768], P('dp'), may hold values from -1.75 to 1.75
- project_weight: bfloat16 [768, 128], P('dp'), may hold values from -0.21875 to 0.21875
- kept_tokens: int32 [8, 2048], P('dp', 'seq'), may hold values 0 or 1
- upstream: float32 [8, 2048, 128], P('dp', 'seq'), may hold values from -96 to 96
Outputs:
- embeddings: float32 [8, 2048, 128], P('dp', 'seq')
- input_grad: float32 [8, 2048, 768], P('dp', 'seq')
- grad_triple: float32 [768, 2304], P('dp')
- grad_queries: float32 [768], P('dp')
- grad_values: float32 [768], P('dp')
- grad_mixer: float32 [768, 768], P('dp')
- grad_offset: float32 [768], P('dp')
- grad_gamma: float32 [768], P('dp')
- grad_beta: float32 [768], P('dp')
- grad_expand: float32 [768, 3072], P('dp')
- grad_lift: float32 [3072], P('dp')
- grad_shrink: float32 [3072, 768], P('dp')
- grad_settle: float32 [768], P('dp')
- grad_gain: float32 [768], P('dp')
- grad_shift: float32 [768], P('dp')
- grad_project: float32 [768, 128], P('dp')
The draws below stay inside these ranges and needn't reach their ends.
All inputs are finite; a program needn't handle non-finite values. No bound on the sum of `kept_tokens` on one device may be relied on, other than what follows from the above.
Results may differ from the reference program's by a relative error of at most 0.018.
Values may be sent and summed in bfloat16 or wider, within the bound.
No kernel may reach another device: no remote copies, remote signals or barrier semaphores. Data moves between devices by JAX's collectives and lax.ppermute only.
A program may use at most 128 MiB of HBM per device.

```python
import jax
import jax.numpy as jnp
from jax import lax

D = 768
H = 12
HD = 64
FF = 3072
EMB = 128
QB = 512
LEN = 2048
SEQS = 8


def set_ends(result, own_key, smallest, high):
    longest = result.shape.index(max(result.shape))
    spots = []
    for shift in (0, 1):
        where = [jax.random.randint(jax.random.fold_in(own_key, axis), (), 0, length) for axis, length in enumerate(result.shape)]
        where[longest] = (where[longest] + shift) % result.shape[longest]
        spots.append(tuple(where))
    return result.at[spots[0]].set(smallest).at[spots[1]].set(high)


def levels(stream_key, dims, split, low, high):
    factor_of = 1.0
    for axis_at, blocks in split:
        draws = jax.random.uniform(jax.random.fold_in(jax.random.fold_in(stream_key, 6), axis_at), (blocks,), jnp.float32, low / len(split), high / len(split))
        factor_of = factor_of * jnp.repeat(jnp.exp(draws), dims[axis_at] // blocks).reshape((-1,) + (1,) * (len(dims) - 1 - axis_at))
    return factor_of


def normal_values(stream_key, extent, width, limit, pieces=(), dtype=jnp.bfloat16):
    values = jax.random.normal(stream_key, extent, jnp.float32) * width
    if len(pieces) > 0:
        values = levels(stream_key, extent, pieces, -0.22, 0.18) * values
    return jnp.clip(values, min=-limit, max=limit).astype(dtype)


def setup_inputs(seed: int = 0) -> dict:
    seeds = jax.random.split(jax.random.key(seed), 18)
    return {
        "layer_input": normal_values(seeds[0], (SEQS, LEN, D), 1.0, 6.0, ((0, 8), (1, 4))),
        "triple_weight": normal_values(seeds[1], (D, 3 * D), D ** -0.5, 0.21875, ((0, 8),)),
        "query_bias": normal_values(seeds[2], (D,), 0.5, 3.0, ((0, 8),)),
        "value_bias": normal_values(seeds[3], (D,), 0.5, 3.0, ((0, 8),)),
        "mixer_weight": normal_values(seeds[4], (D, D), (max(1, D // 384)) ** -0.5, 4.0, ((0, 8),)),
        "mixer_bias": normal_values(seeds[5], (D,), 0.3, 1.75, ((0, 8),)),
        "first_gain": jnp.clip(1.0 + 0.1 * jax.random.normal(seeds[6], (D,), jnp.float32), 0.5, 1.5).astype(jnp.bfloat16),
        "first_shift": normal_values(seeds[7], (D,), 0.3, 1.75, ((0, 8),)),
        "expand_weight": normal_values(seeds[8], (D, FF), D ** -0.5, 0.21875, ((0, 8),)),
        "expand_bias": normal_values(seeds[9], (FF,), 0.3, 1.75, ((0, 8),)),
        "shrink_weight": normal_values(seeds[10], (FF, D), FF ** -0.5, 0.109375, ((0, 8),)),
        "shrink_bias": normal_values(seeds[11], (D,), 0.3, 1.75, ((0, 8),)),
        "second_gain": jnp.clip(1.0 + 0.1 * jax.random.normal(seeds[12], (D,), jnp.float32), 0.5, 1.5).astype(jnp.bfloat16),
        "second_shift": normal_values(seeds[13], (D,), 0.3, 1.75, ((0, 8),)),
        "project_weight": normal_values(seeds[14], (D, EMB), D ** -0.5, 0.21875, ((0, 8),)),
        "kept_tokens": set_ends((jax.random.randint(seeds[15], (SEQS, LEN), 0, 8) < 7).astype(jnp.int32), jax.random.fold_in(seeds[15], 1), 0, 1),
        "upstream": normal_values(seeds[16], (SEQS, LEN, EMB), 16.0, 96.0, ((0, 8), (1, 4)), jnp.float32),
    }


@jax.custom_vjp
def low(v):
    return lax.optimization_barrier(v.astype(jnp.bfloat16)).astype(jnp.float32)

@jax.custom_vjp
def low_back(v):
    return v

def low_keep(v):
    return (low(v), None)

def low_pass(kept, grad):
    return (grad,)

def back_keep(v):
    return (v, None)

def back_low(kept, grad):
    return (low(grad),)
low.defvjp(low_keep, low_pass)
low_back.defvjp(back_keep, back_low)

def layer_norm(rows, gain, shift):
    mean = lax.optimization_barrier(jnp.mean(rows, axis=-1, keepdims=True))
    centred = rows - mean
    spread = lax.optimization_barrier(jnp.mean(centred * centred, axis=-1, keepdims=True))
    return centred * lax.rsqrt(spread + 1e-12) * gain + shift

def unit_rows(rows, keep):
    return rows * lax.rsqrt(lax.optimization_barrier(jnp.sum(rows * rows, axis=-1, keepdims=True)) + 1e-06) * keep

def layer(params, rows, keep):
    triple, qbias, vbias, mixer, mbias, gain_one, shift_one, expand, ebias, shrink, sbias, gain_two, shift_two, project = params
    highest = lax.Precision.HIGHEST
    length = rows.shape[0]
    bias = jnp.concatenate([qbias, jnp.zeros_like(qbias), vbias])
    joined = low_back(low(jnp.dot(rows, triple, precision=highest) + bias))
    query = joined[:, :D].reshape(length, H, HD)
    keys = joined[:, D:2 * D].reshape(length, H, HD)
    values = joined[:, 2 * D:].reshape(length, H, HD)
    blocks = query.reshape(length // QB, QB, H, HD)

    def one_block(qpart):
        scores = low_back(jnp.einsum('qhd,khd->hqk', qpart, keys, precision=highest) * HD ** (-0.5))
        top = lax.optimization_barrier(jnp.max(scores, axis=-1, keepdims=True))
        expo = jnp.exp(scores - top)
        probs = low(expo / lax.optimization_barrier(jnp.sum(expo, axis=-1, keepdims=True)))
        return jnp.einsum('hqk,khd->qhd', probs, values, precision=highest)
    mixed = lax.map(jax.checkpoint(one_block), blocks).reshape(length, D)
    mixed = low_back(low(mixed))
    branch = low_back(jnp.dot(mixed, mixer, precision=highest) + mbias)
    first = layer_norm(rows + branch, gain_one, shift_one)
    lifted = low_back(jnp.dot(low(first), expand, precision=highest) + ebias)
    active = low(jax.nn.gelu(lifted, approximate=False))
    shrunk = low_back(jnp.dot(active, shrink, precision=highest) + sbias)
    second = layer_norm(first + shrunk, gain_two, shift_two)
    projected = low_back(jnp.dot(low(second), project, precision=highest))
    return unit_rows(projected, keep)

def reference(layer_input, triple_weight, query_bias, value_bias, mixer_weight, mixer_bias, first_gain, first_shift, expand_weight, expand_bias, shrink_weight, shrink_bias, second_gain, second_shift, project_weight, kept_tokens, upstream):
    params = tuple((p.astype(jnp.float32) for p in (triple_weight, query_bias, value_bias, mixer_weight, mixer_bias, first_gain, first_shift, expand_weight, expand_bias, shrink_weight, shrink_bias, second_gain, second_shift, project_weight)))

    def one_sequence(totals, items):
        rows, keep, cotangent = items
        embed, back = jax.vjp(lambda p, r: layer(p, r, keep), params, rows.astype(jnp.float32))
        grads, grad_rows = back(cotangent)
        return (jax.tree.map(jnp.add, totals, grads), (embed, grad_rows))
    zeros = jax.tree.map(jnp.zeros_like, params)
    keeps = kept_tokens.astype(jnp.float32)[..., None]
    totals, outputs = lax.scan(one_sequence, zeros, (layer_input, keeps, upstream))
    embeds, grad_rows = outputs
    return (embeds, grad_rows, totals[0], totals[1], totals[2], totals[3], totals[4], totals[5], totals[6], totals[7], totals[8], totals[9], totals[10], totals[11], totals[12], totals[13])
```

```python
import functools

import jax
import jax.numpy as jnp
from jax import lax
from jax.experimental import pallas as pl
from jax.experimental.pallas import tpu as pltpu
from jax.sharding import PartitionSpec as P

HD = 64
LOG2E = 1.4426950408889634
f32 = jnp.float32
bf16 = jnp.bfloat16
NT = (((1,), (1,)), ((), ()))
NN = (((1,), (0,)), ((), ()))
TN = (((0,), (0,)), ((), ()))


def dot(a, b, dims):
    return lax.dot_general(a, b, dims, preferred_element_type=f32)


def attend_forward_kernel(parts, block, heads, *refs):
    joined = refs[:parts]
    mixed_ref, stats_ref = refs[parts:]
    count = joined[0].shape[0]
    for h in range(heads):
        base = 3 * HD * h
        query = joined[block][:, base : base + HD] * jnp.asarray(HD**-0.5, bf16)
        scores = [
            dot(query, j[:, base + HD : base + 2 * HD], NT) * LOG2E for j in joined
        ]
        top = jnp.max(scores[0], axis=1, keepdims=True)
        for s in scores[1:]:
            top = jnp.maximum(top, jnp.max(s, axis=1, keepdims=True))
        total = None
        for s, j in zip(scores, joined):
            probs = jnp.exp2(s - top).astype(bf16)
            wide = jnp.concatenate(
                [j[:, base + 2 * HD : base + 3 * HD], jnp.ones((count, HD), bf16)], axis=1
            )
            part = dot(probs, wide, NN)
            total = part if total is None else total + part
        mass = total[:, HD : HD + 1]
        mixed_ref[:, HD * h : HD * (h + 1)] = (total[:, :HD] / mass).astype(bf16)
        stats_ref[:, h : h + 1] = top + jnp.log2(mass)


def attend_forward(joined, block, heads):
    parts = len(joined)
    count = joined[0].shape[0]
    return pl.pallas_call(
        functools.partial(attend_forward_kernel, parts, block, heads),
        out_shape=[
            jax.ShapeDtypeStruct((count, heads * HD), bf16),
            jax.ShapeDtypeStruct((count, 8), f32),
        ],
        in_specs=[pl.BlockSpec(memory_space=pltpu.VMEM)] * parts,
        out_specs=[pl.BlockSpec(memory_space=pltpu.VMEM)] * 2,
        compiler_params=pltpu.CompilerParams(vmem_limit_bytes=40 << 20),
        cost_estimate=pl.CostEstimate(
            flops=4 * 4 * heads * count * count * parts * HD,
            transcendentals=heads * count * count * parts,
            bytes_accessed=parts * count * heads * HD * 6,
        ),
        name="attend_forward",
    )(*joined)


def attend_backward_kernel(parts, h, *refs):
    joined = refs[:parts]
    grads = refs[parts : 2 * parts]
    mixed = refs[2 * parts : 3 * parts]
    stats = refs[3 * parts : 4 * parts]
    outs = refs[4 * parts : 5 * parts]
    keys_sum, values_sum = refs[5 * parts :]
    base = 3 * HD * h
    count = joined[0].shape[0]
    for b in range(parts):
        query = joined[b][:, base : base + HD] * jnp.asarray(HD**-0.5, bf16)
        grad = grads[b][:, HD * h : HD * (h + 1)]
        inner = jnp.sum(
            grad.astype(f32) * mixed[b][:, HD * h : HD * (h + 1)].astype(f32), axis=1, keepdims=True
        )
        level = stats[b][:, h : h + 1]
        query_t = query.T
        grad_t = grad.T
        total = None
        for c in range(parts):
            keys = joined[c][:, base + HD : base + 2 * HD]
            values = joined[c][:, base + 2 * HD : base + 3 * HD]
            probs = jnp.exp2(dot(query, keys, NT) * LOG2E - level)
            grad_probs = dot(grad, values, NT)
            grad_scores = (probs * (grad_probs - inner)).astype(bf16)
            part = dot(grad_scores, keys, NN)
            total = part if total is None else total + part
            span = slice(c * count, (c + 1) * count)
            grad_values = dot(grad_t, probs.astype(bf16), NN)
            grad_keys = dot(query_t, grad_scores, NN)
            if b == 0:
                values_sum[:, span] = grad_values
                keys_sum[:, span] = grad_keys
            else:
                values_sum[:, span] += grad_values
                keys_sum[:, span] += grad_keys
        outs[b][:, :HD] = (total * HD**-0.5).astype(bf16)
    for c in range(parts):
        span = slice(c * count, (c + 1) * count)
        outs[c][:, HD : 2 * HD] = keys_sum[:, span].T.astype(bf16)
        outs[c][:, 2 * HD :] = values_sum[:, span].T.astype(bf16)


def attend_backward(joined, grads, mixed, stats, h):
    parts = len(joined)
    count = joined[0].shape[0]
    return pl.pallas_call(
        functools.partial(attend_backward_kernel, parts, h),
        out_shape=[jax.ShapeDtypeStruct((count, 3 * HD), bf16)] * parts,
        in_specs=[pl.BlockSpec(memory_space=pltpu.VMEM)] * (4 * parts),
        out_specs=[pl.BlockSpec(memory_space=pltpu.VMEM)] * parts,
        scratch_shapes=[pltpu.VMEM((HD, parts * count), f32)] * 2,
        compiler_params=pltpu.CompilerParams(vmem_limit_bytes=48 << 20),
        cost_estimate=pl.CostEstimate(
            flops=4 * 10 * count * count * parts * parts * HD,
            transcendentals=count * count * parts * parts,
            bytes_accessed=parts * count * HD * 30,
        ),
        name="attend_backward",
    )(*joined, *grads, *mixed, *stats)


def normal_cdf_and_density(x):
    a = jnp.abs(x) * (0.5**0.5)
    t = 1.0 / (1.0 + 0.5 * a)
    series = -0.82215223 + t * 0.17087277
    for c in (1.48851587, -1.13520398, 0.27886807, -0.18628806, 0.09678418, 0.37409196, 1.00002368):
        series = c + t * series
    tail = 0.5 * t * jnp.exp(-a * a - 1.26551223 + t * series)
    cdf = jnp.where(x >= 0, 1.0 - tail, tail)
    return cdf, jnp.exp(-0.5 * x * x) * 0.3989422804014327


def standardize(rows):
    mean = jnp.mean(rows, axis=-1, keepdims=True)
    centred = rows - mean
    spread = jnp.mean(centred * centred, axis=-1, keepdims=True)
    scale = lax.rsqrt(spread + 1e-12)
    return centred * scale, scale


def norm_back(grad, gain, normed, scale):
    g = grad * gain
    return (
        g
        - jnp.mean(g, axis=-1, keepdims=True)
        - normed * jnp.mean(g * normed, axis=-1, keepdims=True)
    ) * scale


def gather(v):
    return lax.all_gather(v, "dp", axis=0, tiled=False)


def send(v, shift):
    if shift == 0:
        return v
    parts = lax.axis_size("seq")
    return lax.ppermute(v, "seq", [(i, (i + shift) % parts) for i in range(parts)])


def rows_of(pieces, dp, width):
    flat = jnp.concatenate(pieces, axis=1)
    pad = -flat.shape[1] % width
    return jnp.pad(flat, ((0, 0), (0, pad))).reshape(dp, -1, width)


def shards(
    layer_input,
    triple_weight,
    query_bias,
    value_bias,
    mixer_weight,
    mixer_bias,
    first_gain,
    first_shift,
    expand_weight,
    expand_bias,
    shrink_weight,
    shrink_bias,
    second_gain,
    second_shift,
    project_weight,
    kept_tokens,
    upstream,
):
    parts = lax.axis_size("seq")
    dp = lax.axis_size("dp")
    place = lax.axis_index("seq")
    mine = lax.axis_index("dp")
    rows = layer_input[0]
    tokens, width = rows.shape
    local = width // parts
    heads = local // HD
    lines = width // dp
    hidden = expand_weight.shape[1]
    hlines = hidden // dp
    emb = project_weight.shape[1]

    blocks = [send(rows, r) for r in range(parts)]

    turned = jnp.roll(
        triple_weight.reshape(lines, 3, parts, heads, HD), -place, axis=2
    ).transpose(0, 2, 3, 1, 4)
    vectors = jnp.concatenate(
        [
            query_bias,
            value_bias,
            mixer_bias,
            first_gain,
            first_shift,
            shrink_bias,
            second_gain,
            second_shift,
            expand_bias,
        ]
    )
    own = gather(
        jnp.concatenate(
            [turned[:, 0].reshape(lines, 3 * local), rows_of([vectors[None]], 1, 3 * local)[0]]
        )
    )
    mixer_project = gather(jnp.concatenate([mixer_weight, project_weight], axis=1))
    w_expand = gather(expand_weight).reshape(width, hidden)
    w_shrink = gather(shrink_weight).reshape(hidden, width)
    w_rest = gather(turned[:, 1:].reshape(lines, (parts - 1) * 3 * local)).reshape(width, -1)

    w_own = own[:, :lines].reshape(width, 3 * local)
    small = own[:, lines:].reshape(dp, -1)
    vec = [small[:, i * lines : (i + 1) * lines].reshape(width).astype(f32) for i in range(8)]
    b_query, b_value, b_mixer, gamma, beta, b_shrink, gain, shift = vec
    b_expand = small[:, 8 * lines : 8 * lines + hlines].reshape(hidden).astype(f32)
    bias = jnp.stack(
        [
            lax.dynamic_slice(b_query, (place * local,), (local,)).reshape(heads, HD),
            jnp.zeros((heads, HD), f32),
            lax.dynamic_slice(b_value, (place * local,), (local,)).reshape(heads, HD),
        ],
        axis=1,
    ).reshape(3 * local)

    joined = [(dot(b, w_own, NN) + bias).astype(bf16) for b in blocks]
    order = list(range(1, parts)) + [0]
    mixed_own = [None] * parts
    stats = [None] * parts
    arrived = [None] * parts
    for r in order:
        mixed_own[r], stats[r] = attend_forward(joined, r, heads)
        arrived[r] = send(mixed_own[r], -r)
    w_mixer = jnp.roll(
        mixer_project[:, :, :width].reshape(parts, local, width), -place, axis=0
    ).reshape(width, width)
    w_project = mixer_project[:, :, width:].reshape(width, emb)
    mixed = jnp.concatenate(arrived, axis=1)

    rows_wide = rows.astype(f32)
    resid_one = rows_wide + (dot(mixed, w_mixer, NN) + b_mixer)
    normed_one, scale_one = standardize(resid_one)
    first = normed_one * gamma + beta
    first_low = first.astype(bf16)
    lifted = dot(first_low, w_expand, NN) + b_expand
    cdf, density = normal_cdf_and_density(lifted)
    active = (lifted * cdf).astype(bf16)
    slope = cdf + lifted * density
    resid_two = first + (dot(active, w_shrink, NN) + b_shrink)
    normed_two, scale_two = standardize(resid_two)
    second_low = (normed_two * gain + shift).astype(bf16)
    projected = dot(second_low, w_project, NN)
    keep = kept_tokens[0].astype(f32)[:, None]
    inverse = lax.rsqrt(jnp.sum(projected * projected, axis=-1, keepdims=True) + 1e-06)
    unit = projected * inverse
    embedded = unit * keep

    ct = upstream[0]
    projected_low = (
        keep * (ct - unit * jnp.sum(unit * ct, axis=-1, keepdims=True)) * inverse
    ).astype(bf16)
    g_project = dot(second_low, projected_low, TN)
    grad_second = dot(projected_low, w_project, NT)
    g_gain = jnp.sum(grad_second * normed_two, axis=0)
    g_shift = jnp.sum(grad_second, axis=0)
    grad_resid_two = norm_back(grad_second, gain, normed_two, scale_two)
    resid_two_low = grad_resid_two.astype(bf16)
    g_settle = jnp.sum(resid_two_low.astype(f32), axis=0)
    g_shrink = dot(active, resid_two_low, TN)
    lifted_low = (dot(resid_two_low, w_shrink, NT) * slope).astype(bf16)
    g_lift = jnp.sum(lifted_low.astype(f32), axis=0)
    g_expand = dot(first_low, lifted_low, TN)
    grad_first = grad_resid_two + dot(lifted_low, w_expand, NT)
    g_gamma = jnp.sum(grad_first * normed_one, axis=0)
    g_beta = jnp.sum(grad_first, axis=0)
    grad_resid_one = norm_back(grad_first, gamma, normed_one, scale_one)
    resid_one_low = grad_resid_one.astype(bf16)
    g_offset = jnp.sum(resid_one_low.astype(f32), axis=0)
    g_mixer = jnp.roll(
        dot(mixed, resid_one_low, TN).reshape(parts, local, width), place, axis=0
    ).reshape(width, width)
    grad_mixed = dot(resid_one_low, w_mixer, NT).astype(bf16)
    grads = [send(grad_mixed[:, r * local : (r + 1) * local], r) for r in range(parts)]

    per = [
        g_shrink.astype(bf16).reshape(dp, hlines, width),
        *[
            g_expand[:, c * width : (c + 1) * width].astype(bf16).reshape(dp, lines, width)
            for c in range(hidden // width)
        ],
        g_mixer.astype(bf16).reshape(dp, lines, width),
        rows_of(
            [g_project.astype(bf16).reshape(dp, lines * emb)]
            + [
                v.astype(bf16).reshape(dp, -1)
                for v in (g_offset, g_gamma, g_beta, g_settle, g_gain, g_shift, g_lift)
            ],
            dp,
            width,
        ),
    ]
    batch = jnp.concatenate(per, axis=1)
    batch = lax.psum_scatter(batch, "dp", scatter_dimension=0, tiled=False)
    batch = lax.psum(batch, "seq").astype(f32)
    at = 0
    r_shrink = batch[:hlines]
    at += hlines
    r_expand = jnp.concatenate(
        [batch[at + c * lines : at + (c + 1) * lines] for c in range(hidden // width)], axis=1
    )
    at += lines * (hidden // width)
    r_mixer = batch[at : at + lines]
    at += lines
    tail = batch[at:].reshape(-1)
    r_project = tail[: lines * emb].reshape(lines, emb)
    at = lines * emb
    r_vec = []
    for _ in range(6):
        r_vec.append(tail[at : at + lines])
        at += lines
    r_offset, r_gamma, r_beta, r_settle, r_gain, r_shift = r_vec
    r_lift = tail[at : at + hlines]

    x_full = jnp.concatenate(blocks, axis=0)
    w_rest = w_rest.reshape(width, parts - 1, heads, 3 * HD)
    input_grad = grad_resid_one
    g_own = []
    for h in range(heads):
        back = attend_backward(joined, grads, mixed_own, stats, h)
        g_own.append(jnp.concatenate(back, axis=0))
        landed = jnp.concatenate([send(back[r], -r) for r in range(parts)], axis=1)
        w_head = jnp.concatenate(
            [
                w_own[:, h * 3 * HD : (h + 1) * 3 * HD],
                w_rest[:, :, h].reshape(width, (parts - 1) * 3 * HD),
            ],
            axis=1,
        )
        input_grad = input_grad + dot(landed, w_head, NT)
    g_own = jnp.concatenate(g_own, axis=1)
    g_triple = dot(x_full, g_own, TN).astype(bf16).reshape(dp, lines, 3 * local)
    columns = jnp.sum(g_own.astype(f32), axis=0).astype(bf16)
    last = jnp.concatenate(
        [g_triple, jnp.broadcast_to(columns, (dp, 1, 3 * local))], axis=1
    )
    last = lax.psum_scatter(last, "dp", scatter_dimension=0, tiled=False)
    last = lax.all_gather(last, "seq", axis=0, tiled=False).astype(f32)
    last = last.reshape(parts, lines + 1, heads, 3, HD).transpose(1, 3, 0, 2, 4)
    r_triple = last[:lines].reshape(lines, 3 * width)
    sums = last[lines].reshape(3, width)
    r_queries = lax.dynamic_slice(sums[0], (mine * lines,), (lines,))
    r_values = lax.dynamic_slice(sums[2], (mine * lines,), (lines,))
    return (
        embedded[None],
        input_grad[None],
        r_triple,
        r_queries,
        r_values,
        r_mixer,
        r_offset,
        r_gamma,
        r_beta,
        r_expand,
        r_lift,
        r_shrink,
        r_settle,
        r_gain,
        r_shift,
        r_project,
    )


def solution(mesh):
    whole = P("dp", "seq", None)
    rows = P("dp", None)
    flat = P("dp")
    in_specs = (
        whole,
        rows,
        flat,
        flat,
        rows,
        flat,
        flat,
        flat,
        rows,
        flat,
        rows,
        flat,
        flat,
        flat,
        rows,
        P("dp", "seq"),
        whole,
    )
    out_specs = (
        whole,
        whole,
        rows,
        flat,
        flat,
        rows,
        flat,
        flat,
        flat,
        rows,
        flat,
        rows,
        flat,
        flat,
        flat,
        rows,
    )
    return jax.shard_map(shards, mesh=mesh, in_specs=in_specs, out_specs=out_specs, check_vma=False)
```

```python
import functools

import jax
import jax.numpy as jnp
from jax import lax
from jax.experimental import pallas as pl
from jax.experimental.pallas import tpu as pltpu
from jax.sharding import PartitionSpec as P

HD = 64
LOG2E = 1.4426950408889634
f32 = jnp.float32
bf16 = jnp.bfloat16
SHORT = pl.CostEstimate(flops=0, transcendentals=0, bytes_accessed=0)
NT = (((1,), (1,)), ((), ()))
NN = (((1,), (0,)), ((), ()))
TN = (((0,), (0,)), ((), ()))


def dot(a, b, dims):
    return lax.dot_general(a, b, dims, preferred_element_type=f32)


def attend_forward_kernel(parts, block, heads, *refs):
    joined = refs[:parts]
    mixed_ref, stats_ref = refs[parts:]
    count = joined[0].shape[0]
    for h in range(heads):
        base = 3 * HD * h
        query = joined[block][:, base : base + HD] * jnp.asarray(HD**-0.5, bf16)
        scores = [
            dot(query, j[:, base + HD : base + 2 * HD], NT) * LOG2E for j in joined
        ]
        top = jnp.max(scores[0], axis=1, keepdims=True)
        for s in scores[1:]:
            top = jnp.maximum(top, jnp.max(s, axis=1, keepdims=True))
        total = None
        for s, j in zip(scores, joined):
            probs = jnp.exp2(s - top).astype(bf16)
            wide = jnp.concatenate(
                [j[:, base + 2 * HD : base + 3 * HD], jnp.ones((count, HD), bf16)], axis=1
            )
            part = dot(probs, wide, NN)
            total = part if total is None else total + part
        mass = total[:, HD : HD + 1]
        mixed_ref[:, HD * h : HD * (h + 1)] = (total[:, :HD] / mass).astype(bf16)
        stats_ref[:, h : h + 1] = top + jnp.log2(mass)


def attend_forward(joined, block, heads):
    parts = len(joined)
    count = joined[0].shape[0]
    return pl.pallas_call(
        functools.partial(attend_forward_kernel, parts, block, heads),
        out_shape=[
            jax.ShapeDtypeStruct((count, heads * HD), bf16),
            jax.ShapeDtypeStruct((count, 8), f32),
        ],
        in_specs=[pl.BlockSpec(memory_space=pltpu.VMEM)] * parts,
        out_specs=[pl.BlockSpec(memory_space=pltpu.VMEM)] * 2,
        compiler_params=pltpu.CompilerParams(vmem_limit_bytes=40 << 20),
        cost_estimate=SHORT,
        name="attend_forward",
    )(*joined)


def attend_backward_kernel(parts, h, *refs):
    joined = refs[:parts]
    grads = refs[parts : 2 * parts]
    mixed = refs[2 * parts : 3 * parts]
    stats = refs[3 * parts : 4 * parts]
    outs = refs[4 * parts : 5 * parts]
    keys_sum, values_sum = refs[5 * parts :]
    base = 3 * HD * h
    count = joined[0].shape[0]
    for b in range(parts):
        query = joined[b][:, base : base + HD] * jnp.asarray(HD**-0.5, bf16)
        grad = grads[b][:, HD * h : HD * (h + 1)]
        inner = jnp.sum(
            grad.astype(f32) * mixed[b][:, HD * h : HD * (h + 1)].astype(f32), axis=1, keepdims=True
        )
        level = stats[b][:, h : h + 1]
        query_t = query.T
        grad_t = grad.T
        total = None
        for c in range(parts):
            keys = joined[c][:, base + HD : base + 2 * HD]
            values = joined[c][:, base + 2 * HD : base + 3 * HD]
            probs = jnp.exp2(dot(query, keys, NT) * LOG2E - level)
            grad_probs = dot(grad, values, NT)
            grad_scores = (probs * (grad_probs - inner)).astype(bf16)
            part = dot(grad_scores, keys, NN)
            total = part if total is None else total + part
            span = slice(c * count, (c + 1) * count)
            grad_values = dot(grad_t, probs.astype(bf16), NN)
            grad_keys = dot(query_t, grad_scores, NN)
            if b == 0:
                values_sum[:, span] = grad_values
                keys_sum[:, span] = grad_keys
            else:
                values_sum[:, span] += grad_values
                keys_sum[:, span] += grad_keys
        outs[b][:, :HD] = (total * HD**-0.5).astype(bf16)
    for c in range(parts):
        span = slice(c * count, (c + 1) * count)
        outs[c][:, HD : 2 * HD] = keys_sum[:, span].T.astype(bf16)
        outs[c][:, 2 * HD :] = values_sum[:, span].T.astype(bf16)


def attend_backward(joined, grads, mixed, stats, h):
    parts = len(joined)
    count = joined[0].shape[0]
    return pl.pallas_call(
        functools.partial(attend_backward_kernel, parts, h),
        out_shape=[jax.ShapeDtypeStruct((count, 3 * HD), bf16)] * parts,
        in_specs=[pl.BlockSpec(memory_space=pltpu.VMEM)] * (4 * parts),
        out_specs=[pl.BlockSpec(memory_space=pltpu.VMEM)] * parts,
        scratch_shapes=[pltpu.VMEM((HD, parts * count), f32)] * 2,
        compiler_params=pltpu.CompilerParams(vmem_limit_bytes=48 << 20),
        cost_estimate=SHORT,
        name="attend_backward",
    )(*joined, *grads, *mixed, *stats)


def normal_cdf_and_density(x):
    a = jnp.abs(x) * (0.5**0.5)
    t = 1.0 / (1.0 + 0.5 * a)
    series = -0.82215223 + t * 0.17087277
    for c in (1.48851587, -1.13520398, 0.27886807, -0.18628806, 0.09678418, 0.37409196, 1.00002368):
        series = c + t * series
    tail = 0.5 * t * jnp.exp(-a * a - 1.26551223 + t * series)
    cdf = jnp.where(x >= 0, 1.0 - tail, tail)
    return cdf, jnp.exp(-0.5 * x * x) * 0.3989422804014327


def standardize(rows):
    mean = jnp.mean(rows, axis=-1, keepdims=True)
    centred = rows - mean
    spread = jnp.mean(centred * centred, axis=-1, keepdims=True)
    scale = lax.rsqrt(spread + 1e-12)
    return centred * scale, scale


def norm_back(grad, gain, normed, scale):
    g = grad * gain
    return (
        g
        - jnp.mean(g, axis=-1, keepdims=True)
        - normed * jnp.mean(g * normed, axis=-1, keepdims=True)
    ) * scale


def ffn_kernel(parts, step, place_ref, *refs):
    rows_ref, arrived, refs = refs[0], refs[1 : 1 + parts], refs[1 + parts :]
    vec_ref, lift_bias_ref, keep_ref, ct_ref, mixer_hbm, expand_hbm, shrink_hbm = refs[:7]
    outs = refs[7:]
    (embedded_ref, resid_ref, first_ref, active_ref, second_ref, plow_ref, two_ref, lifted_ref, one_ref, sums_ref) = outs[:10]
    mixed_grads = outs[10 : 10 + parts]
    mixer_ref, expand_ref, shrink_ref, slope_ref, total_ref, sems = outs[10 + parts :]
    width = rows_ref.shape[1]
    hidden = lift_bias_ref.shape[1]
    local = width // parts
    chunks = hidden // step
    place = place_ref[0]

    load_mixer = pltpu.make_async_copy(mixer_hbm, mixer_ref, sems.at[0])
    load_expand = pltpu.make_async_copy(expand_hbm, expand_ref, sems.at[1])
    load_shrink = pltpu.make_async_copy(shrink_hbm, shrink_ref, sems.at[2])
    load_mixer.start()
    load_expand.start()
    load_shrink.start()

    def vec(i):
        return vec_ref[i : i + 1, :]

    def mixer_rows(r):
        at = lax.rem(place + r, parts) * local
        return mixer_ref[pl.ds(pl.multiple_of(at, local), local), :width]

    load_mixer.wait()
    branch = vec(2)
    for r in range(parts):
        branch = branch + dot(arrived[r][...], mixer_rows(r), NN)
    normed_one, scale_one = standardize(rows_ref[...].astype(f32) + branch)
    first = normed_one * vec(3) + vec(4)
    first_low = first.astype(bf16)
    first_ref[...] = first_low
    total_ref[...] = first + vec(5)

    load_expand.wait()
    load_shrink.wait()

    def forward(c, carry):
        at = pl.multiple_of(c * step, step)
        lifted = dot(first_ref[...], expand_ref[:, pl.ds(at, step)], NN) + lift_bias_ref[:, pl.ds(at, step)]
        cdf, density = normal_cdf_and_density(lifted)
        active = (lifted * cdf).astype(bf16)
        active_ref[:, pl.ds(at, step)] = active
        slope_ref[:, pl.ds(at, step)] = cdf + lifted * density
        total_ref[...] += dot(active, shrink_ref[pl.ds(at, step), :], NN)
        return carry

    lax.fori_loop(0, chunks, forward, 0)

    normed_two, scale_two = standardize(total_ref[...])
    second_low = (normed_two * vec(6) + vec(7)).astype(bf16)
    second_ref[...] = second_low
    w_project = mixer_ref[:, width:]
    projected = dot(second_low, w_project, NN)
    keep = keep_ref[...]
    inverse = lax.rsqrt(jnp.sum(projected * projected, axis=-1, keepdims=True) + 1e-06)
    unit = projected * inverse
    embedded_ref[...] = unit * keep
    ct = ct_ref[...]
    plow = (keep * (ct - unit * jnp.sum(unit * ct, axis=-1, keepdims=True)) * inverse).astype(bf16)
    plow_ref[...] = plow
    grad_second = dot(plow, w_project, NT)
    sums_ref[4:5, :] = jnp.sum(grad_second * normed_two, axis=0, keepdims=True)
    sums_ref[5:6, :] = jnp.sum(grad_second, axis=0, keepdims=True)
    grad_two = norm_back(grad_second, vec(6), normed_two, scale_two)
    two_low = grad_two.astype(bf16)
    two_ref[...] = two_low
    sums_ref[3:4, :] = jnp.sum(two_low.astype(f32), axis=0, keepdims=True)
    total_ref[...] = grad_two

    def backward(c, carry):
        at = pl.multiple_of(c * step, step)
        grad_active = dot(two_ref[...], shrink_ref[pl.ds(at, step), :], NT)
        low = (grad_active * slope_ref[:, pl.ds(at, step)]).astype(bf16)
        lifted_ref[:, pl.ds(at, step)] = low
        total_ref[...] += dot(low, expand_ref[:, pl.ds(at, step)], NT)
        return carry

    lax.fori_loop(0, chunks, backward, 0)
    for c in range(hidden // width):
        sums_ref[6 + c : 7 + c, :] = jnp.sum(
            lifted_ref[:, c * width : (c + 1) * width].astype(f32), axis=0, keepdims=True
        )

    grad_first = total_ref[...]
    sums_ref[1:2, :] = jnp.sum(grad_first * normed_one, axis=0, keepdims=True)
    sums_ref[2:3, :] = jnp.sum(grad_first, axis=0, keepdims=True)
    grad_one = norm_back(grad_first, vec(3), normed_one, scale_one)
    resid_ref[...] = grad_one
    one_low = grad_one.astype(bf16)
    one_ref[...] = one_low
    sums_ref[0:1, :] = jnp.sum(one_low.astype(f32), axis=0, keepdims=True)
    for r in range(parts):
        mixed_grads[r][...] = dot(one_low, mixer_rows(r), NT).astype(bf16)
    used = 6 + hidden // width
    sums_ref[used:, :] = jnp.zeros((sums_ref.shape[0] - used, width), f32)


def feed_forward(place, rows, arrived, vec, lift_bias, keep, ct, mixer, expand, shrink):
    parts = len(arrived)
    tokens, width = rows.shape
    hidden = lift_bias.shape[1]
    emb = ct.shape[1]
    local = width // parts
    V = pl.BlockSpec(memory_space=pltpu.VMEM)
    A = pl.BlockSpec(memory_space=pl.ANY)
    M = pl.BlockSpec(memory_space=pltpu.SMEM)
    S = jax.ShapeDtypeStruct
    return pl.pallas_call(
        functools.partial(ffn_kernel, parts, hidden // 2),
        out_shape=[
            S((tokens, emb), f32),
            S((tokens, width), f32),
            S((tokens, width), bf16),
            S((tokens, hidden), bf16),
            S((tokens, width), bf16),
            S((tokens, emb), bf16),
            S((tokens, width), bf16),
            S((tokens, hidden), bf16),
            S((tokens, width), bf16),
            S((16, width), f32),
        ]
        + [S((tokens, local), bf16)] * parts,
        in_specs=[M, V] + [V] * parts + [V] * 4 + [A] * 3,
        out_specs=[V] * (10 + parts),
        scratch_shapes=[
            pltpu.VMEM((width, width + emb), bf16),
            pltpu.VMEM((width, hidden), bf16),
            pltpu.VMEM((hidden, width), bf16),
            pltpu.VMEM((tokens, hidden), f32),
            pltpu.VMEM((tokens, width), f32),
            pltpu.SemaphoreType.DMA((3,)),
        ],
        compiler_params=pltpu.CompilerParams(vmem_limit_bytes=56 << 20),
        cost_estimate=SHORT,
        name="feed_forward",
    )(place, rows, *arrived, vec, lift_bias, keep, ct, mixer, expand, shrink)


def prepare_kernel(parts, heads, place_ref, triple_ref, *refs):
    vectors, (own_ref, rest_ref) = refs[:-2], refs[-2:]
    lines = triple_ref.shape[0]
    local = heads * HD
    width = parts * local
    shift = lax.rem(parts - place_ref[0], parts) * local
    kinds = [
        pltpu.roll(triple_ref[:, i * width : (i + 1) * width].astype(f32), shift, 1).astype(bf16)
        for i in range(3)
    ]
    for h in range(heads):
        for r in range(parts):
            piece = jnp.concatenate(
                [k[:, r * local + h * HD : r * local + (h + 1) * HD] for k in kinds], axis=1
            )
            if r == 0:
                own_ref[:lines, h * 3 * HD : (h + 1) * 3 * HD] = piece
            else:
                at = (h * (parts - 1) + r - 1) * 3 * HD
                rest_ref[:, at : at + 3 * HD] = piece
    lane = own_ref.shape[1]
    lined = [jnp.zeros((16 - len(vectors), lane), f32)]
    for v in vectors[::-1]:
        line = v[...].astype(f32).reshape(1, -1)
        lined.insert(0, jnp.pad(line, ((0, 0), (0, lane - line.shape[1]))))
    own_ref[lines:, :] = jnp.concatenate(lined).astype(bf16)


def prepare(place, triple, vectors, parts):
    lines, columns = triple.shape
    own = columns // parts
    V = pl.BlockSpec(memory_space=pltpu.VMEM)
    return pl.pallas_call(
        functools.partial(prepare_kernel, parts, own // (3 * HD)),
        out_shape=[
            jax.ShapeDtypeStruct((lines + 16, own), bf16),
            jax.ShapeDtypeStruct((lines, columns - own), bf16),
        ],
        in_specs=[pl.BlockSpec(memory_space=pltpu.SMEM), V] + [V] * len(vectors),
        out_specs=[V] * 2,
        cost_estimate=SHORT,
        name="prepare",
    )(place, triple, *vectors)


def assemble_kernel(parts, origin, place_ref, turn_ref, *refs):
    stacks, (w_ref, bias_ref, vec_ref, lift_ref, all_ref) = refs[:-5], refs[-5:]
    dp = all_ref.shape[0]
    lines = w_ref.shape[0] // dp
    hlines = lift_ref.shape[1] // dp
    width = vec_ref.shape[1]
    local = width // parts
    for stack, ks in zip(stacks, origin):
        for i, k in enumerate(ks):
            s = lax.bitwise_xor(turn_ref[0], k)
            w_ref[pl.ds(pl.multiple_of(s * lines, lines), lines), :] = stack[i, :lines, :]
            all_ref[s] = stack[i, lines:, :].astype(f32)
    vec_ref[...] = jnp.concatenate([all_ref[s][:8, :lines] for s in range(dp)], axis=1)
    lift_ref[...] = jnp.concatenate([all_ref[s][8:9, :hlines] for s in range(dp)], axis=1)
    shift = lax.rem(parts - place_ref[0], parts) * local
    turned = pltpu.roll(vec_ref[...], shift, 1)
    pieces = []
    for at in range(0, local, HD):
        pieces += [turned[0:1, at : at + HD], jnp.zeros((1, HD), f32), turned[1:2, at : at + HD]]
    bias_ref[...] = jnp.concatenate(pieces, axis=1)


def assemble(place, turn, stacks, origin, parts, dp, hidden):
    count, own = stacks[0].shape[1:]
    width = (count - 16) * dp
    V = pl.BlockSpec(memory_space=pltpu.VMEM)
    M = pl.BlockSpec(memory_space=pltpu.SMEM)
    return pl.pallas_call(
        functools.partial(assemble_kernel, parts, origin),
        out_shape=[
            jax.ShapeDtypeStruct((width, own), bf16),
            jax.ShapeDtypeStruct((1, own), f32),
            jax.ShapeDtypeStruct((8, width), f32),
            jax.ShapeDtypeStruct((1, hidden), f32),
        ],
        in_specs=[M, M] + [V] * len(stacks),
        out_specs=[V] * 4,
        scratch_shapes=[pltpu.VMEM((dp, 16, own), f32)],
        cost_estimate=SHORT,
        name="assemble",
    )(place, turn, *stacks)


def input_grad_kernel(parts, heads, resid_ref, own_ref, rest_ref, *refs):
    landed, out_ref = refs[:-1], refs[-1]
    near = jnp.concatenate([landed[h * parts][...] for h in range(heads)], axis=1)
    far = jnp.concatenate(
        [landed[h * parts + r][...] for h in range(heads) for r in range(1, parts)], axis=1
    )
    out_ref[...] = resid_ref[...] + dot(near, own_ref[...], NT) + dot(far, rest_ref[...], NT)


def input_gradient(resid, w_own, w_rest, landed):
    heads, parts = len(landed), len(landed[0])
    V = pl.BlockSpec(memory_space=pltpu.VMEM)
    return pl.pallas_call(
        functools.partial(input_grad_kernel, parts, heads),
        out_shape=jax.ShapeDtypeStruct(resid.shape, f32),
        in_specs=[V] * (3 + heads * parts),
        out_specs=V,
        compiler_params=pltpu.CompilerParams(vmem_limit_bytes=40 << 20),
        cost_estimate=SHORT,
        name="input_gradient",
    )(resid, w_own, w_rest, *[v for h in landed for v in h])


def put(keep_ref, give_ref, k, rows, columns, value):
    place = 2 * lax.bitwise_and(lax.shift_right_logical(k, 1), 1) + lax.shift_right_logical(k, 2)

    @pl.when(lax.bitwise_and(k, 1) == 0)
    def _():
        keep_ref[place, rows, columns] = value

    @pl.when(lax.bitwise_and(k, 1) == 1)
    def _():
        give_ref[place, rows, columns] = value


def weight_grads_kernel(parts, dp, turn_ref, place_ref, *refs):
    arrived = refs[:parts]
    first_ref, active_ref, second_ref, plow_ref, two_ref, lifted_ref, one_ref, sums_ref = refs[parts : parts + 8]
    keep_ref, give_ref = refs[parts + 8 :]
    width = first_ref.shape[1]
    hidden = active_ref.shape[1]
    emb = plow_ref.shape[1]
    lines, hlines, local = width // dp, hidden // dp, width // parts
    turn = turn_ref[0]
    place = place_ref[0]
    every = slice(0, width)

    def store(s, at, count, value, columns=every):
        put(keep_ref, give_ref, lax.bitwise_xor(turn, s), slice(at, at + count), columns, value)

    vectors = sums_ref[...].astype(bf16)
    base_mixer = hlines + lines * (hidden // width)
    base_project = base_mixer + lines
    piece = lines * emb // width
    base_vec = base_project + piece
    two = two_ref[...]
    per = width // hlines
    for c in range(hidden // width):
        part = dot(active_ref[:, c * width : (c + 1) * width], two, TN).astype(bf16)
        for i in range(per):
            store(c * per + i, 0, hlines, part[i * hlines : (i + 1) * hlines])
    first = first_ref[...]
    for c in range(hidden // width):
        part = dot(first, lifted_ref[:, c * width : (c + 1) * width], TN).astype(bf16)
        for s in range(dp):
            store(s, hlines + c * lines, lines, part[s * lines : (s + 1) * lines])
    part = dot(second_ref[...], plow_ref[...], TN).astype(bf16)
    for s in range(dp):
        for a in range(width // emb):
            at = s * lines + a * piece
            store(s, base_project, piece, part[at : at + piece], slice(a * emb, (a + 1) * emb))
        store(s, base_vec, 16, vectors)
    one = one_ref[...]
    per = local // lines
    for r in range(parts):
        part = dot(arrived[r][...], one, TN).astype(bf16)
        j = lax.rem(place + r, parts)
        for i in range(per):
            store(j * per + i, base_mixer, lines, part[i * lines : (i + 1) * lines])


def weight_grads(turn, place, arrived, first, active, second, plow, two, lifted, one, sums, dp):
    parts = len(arrived)
    tokens, width = first.shape
    hidden = active.shape[1]
    emb = plow.shape[1]
    lines, hlines = width // dp, hidden // dp
    total = hlines + lines * (hidden // width) + lines + lines * emb // width + 16
    V = pl.BlockSpec(memory_space=pltpu.VMEM)
    M = pl.BlockSpec(memory_space=pltpu.SMEM)
    return pl.pallas_call(
        functools.partial(weight_grads_kernel, parts, dp),
        out_shape=[jax.ShapeDtypeStruct((dp // 2, total, width), bf16)] * 2,
        in_specs=[M, M] + [V] * (parts + 8),
        out_specs=[V] * 2,
        compiler_params=pltpu.CompilerParams(vmem_limit_bytes=56 << 20),
        cost_estimate=SHORT,
        name="weight_grads",
    )(turn, place, *arrived, first, active, second, plow, two, lifted, one, sums)


def triple_grads_kernel(parts, heads, dp, turn_ref, *refs):
    blocks = refs[:parts]
    backs = refs[parts : parts + heads * parts]
    keep_ref, give_ref = refs[parts + heads * parts :]
    width = blocks[0].shape[1]
    lines = width // dp
    turn = turn_ref[0]
    ones = jnp.ones((16, blocks[0].shape[0]), bf16)
    total = sums = None
    for r in range(parts):
        grad = jnp.concatenate([backs[h * parts + r][...] for h in range(heads)], axis=1)
        part, line = dot(blocks[r][...], grad, TN), dot(ones, grad, NN)
        total = part if r == 0 else total + part
        sums = line if r == 0 else sums + line
    total, sums = total.astype(bf16), sums.astype(bf16)
    columns = slice(0, total.shape[1])
    for s in range(dp):
        k = lax.bitwise_xor(turn, s)
        put(keep_ref, give_ref, k, slice(0, lines), columns, total[s * lines : (s + 1) * lines])
        put(keep_ref, give_ref, k, slice(lines, lines + 16), columns, sums)


def triple_grads(turn, blocks, backs, dp):
    parts, heads = len(blocks), len(backs)
    count, width = blocks[0].shape
    V = pl.BlockSpec(memory_space=pltpu.VMEM)
    return pl.pallas_call(
        functools.partial(triple_grads_kernel, parts, heads, dp),
        out_shape=[jax.ShapeDtypeStruct((dp // 2, width // dp + 16, 3 * HD * heads), bf16)] * 2,
        in_specs=[pl.BlockSpec(memory_space=pltpu.SMEM)] + [V] * (parts + heads * parts),
        out_specs=[V] * 2,
        compiler_params=pltpu.CompilerParams(vmem_limit_bytes=56 << 20),
        cost_estimate=SHORT,
        name="triple_grads",
    )(turn, *blocks, *[b for back in backs for b in back])


def gather(v):
    return lax.all_gather(v, "dp", axis=0, tiled=False)


def send(v, shift):
    if shift == 0:
        return v
    parts = lax.axis_size("seq")
    return lax.ppermute(v, "seq", [(i, (i + shift) % parts) for i in range(parts)])


def hop(v, step):
    parts = lax.axis_size("seq")
    return lax.ppermute(v, "seq", [(i, i + step) for i in range(parts) if 0 <= i + step < parts])


def swap(v, bits):
    return lax.ppermute(v, "dp", [(i, i ^ bits) for i in range(lax.axis_size("dp"))])


def double(v, bits):
    return jnp.concatenate([v, swap(v, bits)])


def after(values, others):
    return lax.optimization_barrier((values, others))[0]


def add(a, b):
    return (a.astype(f32) + b.astype(f32)).astype(bf16)


def sum_dp_core(keep, other):
    half = keep.shape[1] // 32 * 16
    a, b = slice(0, half), slice(half, None)
    pick = lambda rows, *slots: jnp.concatenate(
        [add(keep[i : i + 1, rows], other[i : i + 1, rows]) for i in slots]
    )
    return (pick(a, 0, 1), pick(a, 2, 3), pick(b, 0, 2), pick(b, 1, 3))


def sum_dp_first(sums):
    a_keep, a_give, b_keep, b_give = sums
    return (a_keep, swap(a_give, 2), b_keep, swap(b_give, 4))


def sum_dp_second(sums):
    a_keep, a_came, b_keep, b_came = sums
    a, b = add(a_keep, a_came), add(b_keep, b_came)
    return (a[0], a[1], b[0], b[1])


def sum_dp_last(sums):
    a_keep, a_give, b_keep, b_give = sums
    return (a_keep, swap(a_give, 4), b_keep, swap(b_give, 2))


def sum_dp_short(keep, give):
    total = add(keep, swap(give, 1))
    total = add(total[:2], swap(total[2:], 2))
    return add(total[0], swap(total[1], 4))


def swap_seq(v, bits):
    return lax.ppermute(v, "seq", [(i, i ^ bits) for i in range(lax.axis_size("seq"))])


def turned_seq(items):
    place = lax.axis_index("seq")
    came = jnp.stack(items)
    return [
        lax.dynamic_index_in_dim(came, lax.bitwise_xor(place, k), keepdims=False)
        for k in range(len(items))
    ]


def spread_seq(v):
    two = jnp.stack([v, swap_seq(v, 1)])
    four = jnp.concatenate([two, swap_seq(two, 2)])
    return turned_seq([four[i] for i in range(4)])


def sum_seq_first(v):
    v = v.reshape(4, -1, v.shape[1])
    v = turned_seq([v[i] for i in range(4)])
    came = swap_seq(jnp.stack([v[1], v[3]]), 1)
    return add(v[0], came[0]), add(v[2], came[1])


def sum_seq_second(v):
    return add(v[0], swap_seq(v[1], 2))


def rows_of(pieces, dp, width):
    flat = jnp.concatenate(pieces, axis=1)
    pad = -flat.shape[1] % width
    return jnp.pad(flat, ((0, 0), (0, pad))).reshape(dp, -1, width)


def shards(
    layer_input,
    triple_weight,
    query_bias,
    value_bias,
    mixer_weight,
    mixer_bias,
    first_gain,
    first_shift,
    expand_weight,
    expand_bias,
    shrink_weight,
    shrink_bias,
    second_gain,
    second_shift,
    project_weight,
    kept_tokens,
    upstream,
):
    parts = lax.axis_size("seq")
    dp = lax.axis_size("dp")
    place = lax.axis_index("seq")
    mine = lax.axis_index("dp")
    rows = layer_input[0]
    tokens, width = rows.shape
    local = width // parts
    heads = local // HD
    lines = width // dp
    hidden = expand_weight.shape[1]
    hlines = hidden // dp
    emb = project_weight.shape[1]

    fast = dp == 8 and parts == 4 and heads == 3 and lines % 16 == 0
    if fast:
        below, above = [rows], [rows]
        for _ in range(parts - 1):
            below.append(hop(below[-1], 1))
            above.append(hop(above[-1], -1))
    else:
        blocks = [send(rows, r) for r in range(parts)]

    where = jnp.reshape(place, (1,))
    turn = jnp.reshape(mine, (1,))
    vectors = [
        query_bias,
        value_bias,
        mixer_bias,
        first_gain,
        first_shift,
        shrink_bias,
        second_gain,
        second_shift,
        expand_bias,
    ]
    both = jnp.concatenate([mixer_weight, project_weight], axis=1)
    if fast:
        own, rest = prepare(where, triple_weight, vectors, parts)
        own = double(own[None], 2)
        own = [own, swap(own, 4)]
        own, below, above = lax.optimization_barrier((own, below, above))
        blocks = [rows] + [
            jnp.where(place >= r, below[r], above[parts - r]) for r in range(1, parts)
        ]
        own += [swap(w, 1) for w in own]
        origin = [(0, 2), (4, 6), (1, 3), (5, 7)]
        w_own, bias, vec, b_expand = assemble(where, turn, own, origin, parts, dp, hidden)
        w_rest = gather(rest).reshape(width, -1)
    else:
        turned = jnp.roll(
            triple_weight.reshape(lines, 3, parts, heads, HD), -place, axis=2
        ).transpose(0, 2, 3, 1, 4)
        w_own = gather(turned[:, 0].reshape(lines, 3 * local)).reshape(width, 3 * local)
        w_rest = gather(turned[:, 1:].swapaxes(1, 2).reshape(lines, -1)).reshape(width, -1)
        small = gather(jnp.concatenate(vectors)).astype(f32)
        vec = jnp.stack([small[:, i * lines : (i + 1) * lines].reshape(width) for i in range(8)])
        b_expand = small[:, 8 * lines :].reshape(1, hidden)
        b_query, b_value = [
            lax.dynamic_slice(vec[i], (place * local,), (local,)).reshape(heads, HD) for i in (0, 1)
        ]
        bias = jnp.stack([b_query, jnp.zeros((heads, HD), f32), b_value], axis=1).reshape(1, -1)
    both = gather(both).reshape(width, width + emb)
    w_expand = gather(expand_weight).reshape(width, hidden)
    w_shrink = gather(shrink_weight).reshape(hidden, width)

    joined = [(dot(b, w_own, NN) + bias).astype(bf16) for b in blocks]
    order = list(range(2, parts)) + [1, 0]
    mixed_own = [None] * parts
    stats = [None] * parts
    arrived = [None] * parts
    for i, r in enumerate(order):
        if i > 0:
            joined = after(joined, mixed_own[order[i - 1]])
        mixed_own[r], stats[r] = attend_forward(joined, r, heads)
        arrived[r] = send(mixed_own[r], -r)
    results = feed_forward(
        where,
        rows,
        arrived,
        vec,
        b_expand,
        kept_tokens[0].astype(f32)[:, None],
        upstream[0],
        both,
        w_expand,
        w_shrink,
    )
    embedded, grad_resid_one, first, active, second, plow, two, lifted, one, sums = results[:10]
    grads = [send(g, r) for r, g in enumerate(results[10:])]

    slabs = hidden // width
    backs = []
    landed = []
    inputs = (joined, grads, mixed_own, stats)

    def backward(h, inputs):
        back = attend_backward(*inputs, h)
        backs.append(back)
        landed.append([send(back[r], -r) for r in range(parts)])

    if fast:
        first, w_rest = lax.optimization_barrier((first, w_rest))
        keep, give = weight_grads(
            turn, where, arrived, first, active, second, plow, two, lifted, one, sums, dp
        )
        grads, give = lax.optimization_barrier((grads, give))
        other = swap(give, 1)
        inputs = after((joined, grads, mixed_own, stats), keep)
        backward(0, inputs)
        batch = sum_dp_core(*after((keep, other), backs[0]))
        inputs = after(inputs, batch)
        batch = sum_dp_first(batch)
        backward(1, inputs)
        backward(2, after(inputs, (landed[0], backs[1])))
        batch = sum_dp_second(after(batch, (landed[1], backs[2])))
        backs = after(backs, batch)
        batch = sum_dp_last(batch)
        last = triple_grads(turn, blocks, backs, dp)
        batch = after(batch, last)
        batch = jnp.concatenate([add(batch[0], batch[1]), add(batch[2], batch[3])])
        batch = sum_seq_first(batch)
        batch, landed[2] = lax.optimization_barrier((batch, landed[2]))
        batch = sum_seq_second(batch)
        last = sum_dp_short(*last)
        last = spread_seq(last)
        batch = jnp.concatenate(spread_seq(batch))
        last = jnp.stack(last)[:, : lines + 1]
    else:
        g_expand = dot(first, lifted, TN).astype(bf16)
        mixed = jnp.concatenate(arrived, axis=1)
        g_mixer = jnp.roll(dot(mixed, one, TN).reshape(parts, local, width), place, axis=0)
        g_project = dot(second, plow, TN).astype(bf16)
        batch = jnp.concatenate(
            [
                dot(active, two, TN).astype(bf16).reshape(dp, hlines, width),
                *[
                    g_expand[:, c * width : (c + 1) * width].reshape(dp, lines, width)
                    for c in range(slabs)
                ],
                g_mixer.astype(bf16).reshape(dp, lines, width),
                jnp.stack([rows_of([g[None].reshape(1, -1)], 1, width)[0] for g in g_project.reshape(dp, lines, emb)]),
                jnp.broadcast_to(sums.astype(bf16), (dp,) + sums.shape),
            ],
            axis=1,
        )
        batch = lax.psum_scatter(batch, "dp", scatter_dimension=0, tiled=False)
        batch = lax.psum(batch, "seq")
        for h in range(heads):
            backward(h, inputs)
        g_own = jnp.concatenate([jnp.concatenate(back, axis=0) for back in backs], axis=1)
        g_triple = dot(jnp.concatenate(blocks, axis=0), g_own, TN)
        columns = jnp.sum(g_own.astype(f32), axis=0).astype(bf16)
        last = jnp.concatenate(
            [
                g_triple.astype(bf16).reshape(dp, lines, 3 * local),
                jnp.broadcast_to(columns, (dp, 1, 3 * local)),
            ],
            axis=1,
        )
        last = lax.psum_scatter(last, "dp", scatter_dimension=0, tiled=False)
        last = lax.all_gather(last, "seq", axis=0, tiled=False)
    batch = batch.astype(f32)
    r_shrink = batch[:hlines]
    at = hlines
    r_expand = jnp.concatenate(
        [batch[at + c * lines : at + (c + 1) * lines] for c in range(slabs)], axis=1
    )
    at += lines * slabs
    r_mixer = batch[at : at + lines]
    at += lines
    piece = lines * emb // width
    if fast:
        r_project = jnp.concatenate(
            [batch[at : at + piece, a * emb : (a + 1) * emb] for a in range(width // emb)]
        )
    else:
        r_project = batch[at : at + piece].reshape(lines, emb)
    tail = batch[at + piece :]
    r_offset, r_gamma, r_beta, r_settle, r_gain, r_shift = [
        lax.dynamic_slice(tail[i], (mine * lines,), (lines,)) for i in range(6)
    ]
    r_lift = lax.dynamic_slice(
        tail[6 : 6 + slabs].reshape(hidden), (mine * hlines,), (hlines,)
    )

    input_grad = input_gradient(grad_resid_one, w_own, w_rest, landed)
    last = last.astype(f32)
    last = last.reshape(parts, lines + 1, heads, 3, HD).transpose(1, 3, 0, 2, 4)
    r_triple = last[:lines].reshape(lines, 3 * width)
    sums = last[lines].reshape(3, width)
    r_queries = lax.dynamic_slice(sums[0], (mine * lines,), (lines,))
    r_values = lax.dynamic_slice(sums[2], (mine * lines,), (lines,))
    return (
        embedded[None],
        input_grad[None],
        r_triple,
        r_queries,
        r_values,
        r_mixer,
        r_offset,
        r_gamma,
        r_beta,
        r_expand,
        r_lift,
        r_shrink,
        r_settle,
        r_gain,
        r_shift,
        r_project,
    )


def solution(mesh):
    whole = P("dp", "seq", None)
    rows = P("dp", None)
    flat = P("dp")
    in_specs = (
        whole,
        rows,
        flat,
        flat,
        rows,
        flat,
        flat,
        flat,
        rows,
        flat,
        rows,
        flat,
        flat,
        flat,
        rows,
        P("dp", "seq"),
        whole,
    )
    out_specs = (
        whole,
        whole,
        rows,
        flat,
        flat,
        rows,
        flat,
        flat,
        flat,
        rows,
        flat,
        rows,
        flat,
        flat,
        flat,
        rows,
    )
    return jax.shard_map(shards, mesh=mesh, in_specs=in_specs, out_specs=out_specs, check_vma=False)
```

```python
import functools

import jax
import jax.numpy as jnp
from jax import lax
from jax.experimental import pallas as pl
from jax.experimental.pallas import tpu as pltpu
from jax.sharding import PartitionSpec as P

HD = 64
LOG2E = 1.4426950408889634
f32 = jnp.float32
bf16 = jnp.bfloat16
SHORT = pl.CostEstimate(flops=0, transcendentals=0, bytes_accessed=0)
NT = (((1,), (1,)), ((), ()))
NN = (((1,), (0,)), ((), ()))
TN = (((0,), (0,)), ((), ()))


def dot(a, b, dims):
    return lax.dot_general(a, b, dims, preferred_element_type=f32)


def attend_forward_kernel(parts, block, heads, *refs):
    joined = refs[:parts]
    mixed_ref, stats_ref = refs[parts:]
    count = joined[0].shape[0]
    for h in range(heads):
        base = 3 * HD * h
        query = joined[block][:, base : base + HD] * jnp.asarray(HD**-0.5, bf16)
        scores = [
            dot(query, j[:, base + HD : base + 2 * HD], NT) * LOG2E for j in joined
        ]
        top = jnp.max(scores[0], axis=1, keepdims=True)
        for s in scores[1:]:
            top = jnp.maximum(top, jnp.max(s, axis=1, keepdims=True))
        total = None
        for s, j in zip(scores, joined):
            probs = jnp.exp2(s - top).astype(bf16)
            wide = jnp.concatenate(
                [j[:, base + 2 * HD : base + 3 * HD], jnp.ones((count, HD), bf16)], axis=1
            )
            part = dot(probs, wide, NN)
            total = part if total is None else total + part
        mass = total[:, HD : HD + 1]
        mixed_ref[:, HD * h : HD * (h + 1)] = (total[:, :HD] / mass).astype(bf16)
        stats_ref[:, h : h + 1] = top + jnp.log2(mass)


def attend_forward(joined, block, heads):
    parts = len(joined)
    count = joined[0].shape[0]
    return pl.pallas_call(
        functools.partial(attend_forward_kernel, parts, block, heads),
        out_shape=[
            jax.ShapeDtypeStruct((count, heads * HD), bf16),
            jax.ShapeDtypeStruct((count, 8), f32),
        ],
        in_specs=[pl.BlockSpec(memory_space=pltpu.VMEM)] * parts,
        out_specs=[pl.BlockSpec(memory_space=pltpu.VMEM)] * 2,
        compiler_params=pltpu.CompilerParams(vmem_limit_bytes=40 << 20),
        cost_estimate=SHORT,
        name="attend_forward",
    )(*joined)


def attend_backward_kernel(parts, h, *refs):
    joined = refs[:parts]
    grads = refs[parts : 2 * parts]
    mixed = refs[2 * parts : 3 * parts]
    stats = refs[3 * parts : 4 * parts]
    outs = refs[4 * parts : 5 * parts]
    keys_sum, values_sum = refs[5 * parts :]
    base = 3 * HD * h
    count = joined[0].shape[0]
    for b in range(parts):
        query = joined[b][:, base : base + HD] * jnp.asarray(HD**-0.5, bf16)
        grad = grads[b][:, HD * h : HD * (h + 1)]
        inner = jnp.sum(
            grad.astype(f32) * mixed[b][:, HD * h : HD * (h + 1)].astype(f32), axis=1, keepdims=True
        )
        level = stats[b][:, h : h + 1]
        query_t = query.T
        grad_t = grad.T
        total = None
        for c in range(parts):
            keys = joined[c][:, base + HD : base + 2 * HD]
            values = joined[c][:, base + 2 * HD : base + 3 * HD]
            probs = jnp.exp2(dot(query, keys, NT) * LOG2E - level)
            grad_probs = dot(grad, values, NT)
            grad_scores = (probs * (grad_probs - inner)).astype(bf16)
            part = dot(grad_scores, keys, NN)
            total = part if total is None else total + part
            span = slice(c * count, (c + 1) * count)
            grad_values = dot(grad_t, probs.astype(bf16), NN)
            grad_keys = dot(query_t, grad_scores, NN)
            if b == 0:
                values_sum[:, span] = grad_values
                keys_sum[:, span] = grad_keys
            else:
                values_sum[:, span] += grad_values
                keys_sum[:, span] += grad_keys
        outs[b][:, :HD] = (total * HD**-0.5).astype(bf16)
    for c in range(parts):
        span = slice(c * count, (c + 1) * count)
        outs[c][:, HD : 2 * HD] = keys_sum[:, span].T.astype(bf16)
        outs[c][:, 2 * HD :] = values_sum[:, span].T.astype(bf16)


def attend_backward(joined, grads, mixed, stats, h):
    parts = len(joined)
    count = joined[0].shape[0]
    return pl.pallas_call(
        functools.partial(attend_backward_kernel, parts, h),
        out_shape=[jax.ShapeDtypeStruct((count, 3 * HD), bf16)] * parts,
        grid=(1,),
        scratch_shapes=[pltpu.VMEM((HD, parts * count), f32)] * 2,
        compiler_params=pltpu.CompilerParams(vmem_limit_bytes=60 << 20),
        cost_estimate=SHORT,
        name="attend_backward",
    )(*joined, *grads, *mixed, *stats)


def normal_cdf_and_density(x):
    a = jnp.abs(x) * (0.5**0.5)
    t = 1.0 / (1.0 + 0.5 * a)
    series = -0.82215223 + t * 0.17087277
    for c in (1.48851587, -1.13520398, 0.27886807, -0.18628806, 0.09678418, 0.37409196, 1.00002368):
        series = c + t * series
    tail = 0.5 * t * jnp.exp(-a * a - 1.26551223 + t * series)
    cdf = jnp.where(x >= 0, 1.0 - tail, tail)
    return cdf, jnp.exp(-0.5 * x * x) * 0.3989422804014327


def standardize(rows):
    mean = jnp.mean(rows, axis=-1, keepdims=True)
    centred = rows - mean
    spread = jnp.mean(centred * centred, axis=-1, keepdims=True)
    scale = lax.rsqrt(spread + 1e-12)
    return centred * scale, scale


def norm_back(grad, gain, normed, scale):
    g = grad * gain
    return (
        g
        - jnp.mean(g, axis=-1, keepdims=True)
        - normed * jnp.mean(g * normed, axis=-1, keepdims=True)
    ) * scale


def ffn_kernel(parts, step, wide_from, shrink_from, place_ref, turn_ref, *refs):
    rows_ref, arrived, refs = refs[0], refs[1 : 1 + parts], refs[1 + parts :]
    vec_ref, lift_bias_ref, keep_ref, ct_ref = refs[:4]
    groups = len(wide_from)
    wide_hbm, shrink_hbm = refs[4 : 4 + groups], refs[4 + groups : 4 + 2 * groups]
    outs = refs[4 + 2 * groups :]
    (embedded_ref, resid_ref, first_ref, active_ref, second_ref, plow_ref, two_ref, lifted_ref, one_ref, sums_ref) = outs[:10]
    mixed_grads = outs[10 : 10 + parts]
    mixer_ref, expand_ref, shrink_ref, slope_ref, total_ref, sems = outs[10 + parts :]
    width = rows_ref.shape[1]
    hidden = lift_bias_ref.shape[1]
    local = width // parts
    chunks = hidden // step
    place = place_ref[0]

    pieces = sum(len(f) for f in wide_from)

    def load(sources, origin, columns, target, first):
        count = target.shape[0] // pieces
        copies = []
        for source, ks in zip(sources, origin):
            for i, k in enumerate(ks):
                at = pl.multiple_of(lax.bitwise_xor(turn_ref[0], k) * count, count) if pieces > 1 else 0
                copies.append(
                    pltpu.make_async_copy(
                        source.at[i, :, columns],
                        target.at[pl.ds(at, count), :],
                        sems.at[first + len(copies)],
                    )
                )
                copies[-1].start()
        return copies

    side = width + ct_ref.shape[1]
    load_mixer = load(wide_hbm, wide_from, slice(hidden, hidden + side), mixer_ref, 0)
    load_expand = load(wide_hbm, wide_from, slice(0, hidden), expand_ref, pieces)
    load_shrink = load(shrink_hbm, shrink_from, slice(0, width), shrink_ref, 2 * pieces)

    def vec(i):
        return vec_ref[i : i + 1, :]

    def mixer_rows(r):
        at = lax.rem(place + r, parts) * local
        return mixer_ref[pl.ds(pl.multiple_of(at, local), local), :width]

    for copy in load_mixer:
        copy.wait()
    branch = vec(2)
    for r in range(parts):
        branch = branch + dot(arrived[r][...], mixer_rows(r), NN)
    normed_one, scale_one = standardize(rows_ref[...].astype(f32) + branch)
    first = normed_one * vec(3) + vec(4)
    first_low = first.astype(bf16)
    first_ref[...] = first_low
    total_ref[...] = first + vec(5)

    for copy in load_expand + load_shrink:
        copy.wait()

    def forward(c, carry):
        at = pl.multiple_of(c * step, step)
        lifted = dot(first_ref[...], expand_ref[:, pl.ds(at, step)], NN) + lift_bias_ref[:, pl.ds(at, step)]
        cdf, density = normal_cdf_and_density(lifted)
        active = (lifted * cdf).astype(bf16)
        active_ref[:, pl.ds(at, step)] = active
        slope_ref[:, pl.ds(at, step)] = cdf + lifted * density
        total_ref[...] += dot(active, shrink_ref[pl.ds(at, step), :], NN)
        return carry

    lax.fori_loop(0, chunks, forward, 0)

    normed_two, scale_two = standardize(total_ref[...])
    second_low = (normed_two * vec(6) + vec(7)).astype(bf16)
    second_ref[...] = second_low
    w_project = mixer_ref[:, width:]
    projected = dot(second_low, w_project, NN)
    keep = keep_ref[...]
    inverse = lax.rsqrt(jnp.sum(projected * projected, axis=-1, keepdims=True) + 1e-06)
    unit = projected * inverse
    embedded_ref[...] = unit * keep
    ct = ct_ref[...]
    plow = (keep * (ct - unit * jnp.sum(unit * ct, axis=-1, keepdims=True)) * inverse).astype(bf16)
    plow_ref[...] = plow
    grad_second = dot(plow, w_project, NT)
    sums_ref[4:5, :] = jnp.sum(grad_second * normed_two, axis=0, keepdims=True)
    sums_ref[5:6, :] = jnp.sum(grad_second, axis=0, keepdims=True)
    grad_two = norm_back(grad_second, vec(6), normed_two, scale_two)
    two_low = grad_two.astype(bf16)
    two_ref[...] = two_low
    sums_ref[3:4, :] = jnp.sum(two_low.astype(f32), axis=0, keepdims=True)
    total_ref[...] = grad_two

    def backward(c, carry):
        at = pl.multiple_of(c * step, step)
        grad_active = dot(two_ref[...], shrink_ref[pl.ds(at, step), :], NT)
        low = (grad_active * slope_ref[:, pl.ds(at, step)]).astype(bf16)
        lifted_ref[:, pl.ds(at, step)] = low
        total_ref[...] += dot(low, expand_ref[:, pl.ds(at, step)], NT)
        return carry

    lax.fori_loop(0, chunks, backward, 0)
    for c in range(hidden // width):
        sums_ref[6 + c : 7 + c, :] = jnp.sum(
            lifted_ref[:, c * width : (c + 1) * width].astype(f32), axis=0, keepdims=True
        )

    grad_first = total_ref[...]
    sums_ref[1:2, :] = jnp.sum(grad_first * normed_one, axis=0, keepdims=True)
    sums_ref[2:3, :] = jnp.sum(grad_first, axis=0, keepdims=True)
    grad_one = norm_back(grad_first, vec(3), normed_one, scale_one)
    resid_ref[...] = grad_one
    one_low = grad_one.astype(bf16)
    one_ref[...] = one_low
    sums_ref[0:1, :] = jnp.sum(one_low.astype(f32), axis=0, keepdims=True)
    for r in range(parts):
        mixed_grads[r][...] = dot(one_low, mixer_rows(r), NT).astype(bf16)
    used = 6 + hidden // width
    sums_ref[used:, :] = jnp.zeros((sums_ref.shape[0] - used, width), f32)


def feed_forward(place, turn, rows, arrived, vec, lift_bias, keep, ct, wide, wide_from, shrink, shrink_from):
    parts = len(arrived)
    groups = len(wide)
    pieces = sum(len(f) for f in wide_from)
    tokens, width = rows.shape
    hidden = lift_bias.shape[1]
    emb = ct.shape[1]
    local = width // parts
    V = pl.BlockSpec(memory_space=pltpu.VMEM)
    A = pl.BlockSpec(memory_space=pl.ANY)
    M = pl.BlockSpec(memory_space=pltpu.SMEM)
    S = jax.ShapeDtypeStruct
    return pl.pallas_call(
        functools.partial(ffn_kernel, parts, hidden // 2, wide_from, shrink_from),
        out_shape=[
            S((tokens, emb), f32),
            S((tokens, width), f32),
            S((tokens, width), bf16),
            S((tokens, hidden), bf16),
            S((tokens, width), bf16),
            S((tokens, emb), bf16),
            S((tokens, width), bf16),
            S((tokens, hidden), bf16),
            S((tokens, width), bf16),
            S((16, width), f32),
        ]
        + [S((tokens, local), bf16)] * parts,
        in_specs=[M, M, V] + [V] * parts + [V] * 4 + [A] * (2 * groups),
        out_specs=[V] * (10 + parts),
        scratch_shapes=[
            pltpu.VMEM((width, width + emb), bf16),
            pltpu.VMEM((width, hidden), bf16),
            pltpu.VMEM((hidden, width), bf16),
            pltpu.VMEM((tokens, hidden), f32),
            pltpu.VMEM((tokens, width), f32),
            pltpu.SemaphoreType.DMA((3 * pieces,)),
        ],
        compiler_params=pltpu.CompilerParams(vmem_limit_bytes=56 << 20),
        cost_estimate=SHORT,
        name="feed_forward",
    )(place, turn, rows, *arrived, vec, lift_bias, keep, ct, *wide, *shrink)


def prepare_kernel(parts, heads, place_ref, triple_ref, *refs):
    vectors, (own_ref, rest_ref) = refs[:-2], refs[-2:]
    lines = triple_ref.shape[0]
    local = heads * HD
    width = parts * local
    shift = lax.rem(parts - place_ref[0], parts) * local
    kinds = [
        pltpu.roll(triple_ref[:, i * width : (i + 1) * width].astype(f32), shift, 1).astype(bf16)
        for i in range(3)
    ]
    for h in range(heads):
        for r in range(parts):
            piece = jnp.concatenate(
                [k[:, r * local + h * HD : r * local + (h + 1) * HD] for k in kinds], axis=1
            )
            if r == 0:
                own_ref[:lines, h * 3 * HD : (h + 1) * 3 * HD] = piece
            else:
                at = (h * (parts - 1) + r - 1) * 3 * HD
                rest_ref[:, at : at + 3 * HD] = piece
    lane = own_ref.shape[1]
    lined = [jnp.zeros((16 - len(vectors), lane), f32)]
    for v in vectors[::-1]:
        line = v[...].astype(f32).reshape(1, -1)
        lined.insert(0, jnp.pad(line, ((0, 0), (0, lane - line.shape[1]))))
    own_ref[lines:, :] = jnp.concatenate(lined).astype(bf16)


def prepare(place, triple, vectors, parts):
    lines, columns = triple.shape
    own = columns // parts
    V = pl.BlockSpec(memory_space=pltpu.VMEM)
    return pl.pallas_call(
        functools.partial(prepare_kernel, parts, own // (3 * HD)),
        out_shape=[
            jax.ShapeDtypeStruct((lines + 16, own), bf16),
            jax.ShapeDtypeStruct((lines, columns - own), bf16),
        ],
        in_specs=[pl.BlockSpec(memory_space=pltpu.SMEM), V] + [V] * len(vectors),
        out_specs=[V] * 2,
        cost_estimate=SHORT,
        name="prepare",
    )(place, triple, *vectors)


def assemble_kernel(parts, origin, place_ref, turn_ref, *refs):
    stacks, (w_ref, bias_ref, vec_ref, lift_ref, all_ref) = refs[:-5], refs[-5:]
    dp = all_ref.shape[0]
    lines = w_ref.shape[0] // dp
    hlines = lift_ref.shape[1] // dp
    width = vec_ref.shape[1]
    local = width // parts
    for stack, ks in zip(stacks, origin):
        for i, k in enumerate(ks):
            s = lax.bitwise_xor(turn_ref[0], k)
            w_ref[pl.ds(pl.multiple_of(s * lines, lines), lines), :] = stack[i, :lines, :]
            all_ref[s] = stack[i, lines:, :].astype(f32)
    vec_ref[...] = jnp.concatenate([all_ref[s][:8, :lines] for s in range(dp)], axis=1)
    lift_ref[...] = jnp.concatenate([all_ref[s][8:9, :hlines] for s in range(dp)], axis=1)
    shift = lax.rem(parts - place_ref[0], parts) * local
    turned = pltpu.roll(vec_ref[...], shift, 1)
    pieces = []
    for at in range(0, local, HD):
        pieces += [turned[0:1, at : at + HD], jnp.zeros((1, HD), f32), turned[1:2, at : at + HD]]
    bias_ref[...] = jnp.concatenate(pieces, axis=1)


def assemble(place, turn, stacks, origin, parts, dp, hidden):
    count, own = stacks[0].shape[1:]
    width = (count - 16) * dp
    V = pl.BlockSpec(memory_space=pltpu.VMEM)
    M = pl.BlockSpec(memory_space=pltpu.SMEM)
    return pl.pallas_call(
        functools.partial(assemble_kernel, parts, origin),
        out_shape=[
            jax.ShapeDtypeStruct((width, own), bf16),
            jax.ShapeDtypeStruct((1, own), f32),
            jax.ShapeDtypeStruct((8, width), f32),
            jax.ShapeDtypeStruct((1, hidden), f32),
        ],
        in_specs=[M, M] + [V] * len(stacks),
        out_specs=[V] * 4,
        scratch_shapes=[pltpu.VMEM((dp, 16, own), f32)],
        cost_estimate=SHORT,
        name="assemble",
    )(place, turn, *stacks)


def input_grad_kernel(origin, parts, heads, turn_ref, resid_ref, own_ref, *refs):
    landed, refs = refs[: heads * parts], refs[heads * parts :]
    stacks, (out_ref, rest_ref) = refs[: len(origin)], refs[len(origin) :]
    pieces = sum(len(ks) for ks in origin)
    count = rest_ref.shape[0] // pieces
    for source, ks in zip(stacks, origin):
        for i, k in enumerate(ks):
            at = pl.multiple_of(lax.bitwise_xor(turn_ref[0], k) * count, count) if pieces > 1 else 0
            rest_ref[pl.ds(at, count), :] = source[i]
    near = jnp.concatenate([landed[h * parts][...] for h in range(heads)], axis=1)
    far = jnp.concatenate(
        [landed[h * parts + r][...] for h in range(heads) for r in range(1, parts)], axis=1
    )
    out_ref[...] = resid_ref[...] + dot(near, own_ref[...], NT) + dot(far, rest_ref[...], NT)


def input_gradient(turn, resid, w_own, landed, stacks, origin):
    heads, parts = len(landed), len(landed[0])
    W = pl.BlockSpec()
    return pl.pallas_call(
        functools.partial(input_grad_kernel, origin, parts, heads),
        grid=(1,),
        out_shape=jax.ShapeDtypeStruct(resid.shape, f32),
        in_specs=[pl.BlockSpec(memory_space=pltpu.SMEM)] + [W] * (2 + heads * parts + len(stacks)),
        out_specs=W,
        scratch_shapes=[pltpu.VMEM((resid.shape[1], stacks[0].shape[2]), bf16)],
        compiler_params=pltpu.CompilerParams(vmem_limit_bytes=60 << 20),
        cost_estimate=SHORT,
        name="input_gradient",
    )(turn, resid, w_own, *[v for h in landed for v in h], *stacks)


def put(keep_ref, give_ref, k, rows, columns, value):
    place = 2 * lax.bitwise_and(lax.shift_right_logical(k, 1), 1) + lax.shift_right_logical(k, 2)

    @pl.when(lax.bitwise_and(k, 1) == 0)
    def _():
        keep_ref[place, rows, columns] = value

    @pl.when(lax.bitwise_and(k, 1) == 1)
    def _():
        give_ref[place, rows, columns] = value


def weight_grads_kernel(parts, dp, turn_ref, place_ref, *refs):
    arrived = refs[:parts]
    first_ref, active_ref, second_ref, plow_ref, two_ref, lifted_ref, one_ref, sums_ref = refs[parts : parts + 8]
    keep_ref, give_ref, out_ref, sems = refs[parts + 8 :]
    width = first_ref.shape[1]
    hidden = active_ref.shape[1]
    emb = plow_ref.shape[1]
    lines, hlines, local = width // dp, hidden // dp, width // parts
    turn = turn_ref[0]
    place = place_ref[0]
    slabs = hidden // width
    base_mixer = hlines + lines * slabs
    base_project = base_mixer + lines
    piece = lines * emb // width
    base_vec = base_project + piece

    def leave(stage, at, count):
        for s in range(dp):
            k = lax.bitwise_xor(turn, s)
            slot = 2 * lax.bitwise_and(lax.shift_right_logical(k, 1), 1) + lax.shift_right_logical(k, 2)
            source = out_ref.at[s, pl.ds(at, count)]
            sem = sems.at[stage, s]

            @pl.when(lax.bitwise_and(k, 1) == 0)
            def _():
                pltpu.make_async_copy(source, keep_ref.at[slot, pl.ds(at, count)], sem).start()

            @pl.when(lax.bitwise_and(k, 1) == 1)
            def _():
                pltpu.make_async_copy(source, give_ref.at[slot, pl.ds(at, count)], sem).start()

    two = two_ref[...]
    per = width // hlines
    for c in range(slabs):
        part = dot(active_ref[:, c * width : (c + 1) * width], two, TN).astype(bf16)
        for i in range(per):
            out_ref[c * per + i, :hlines, :] = part[i * hlines : (i + 1) * hlines]
    leave(0, 0, hlines)
    first = first_ref[...]
    for c in range(slabs):
        part = dot(first, lifted_ref[:, c * width : (c + 1) * width], TN).astype(bf16)
        at = hlines + c * lines
        for s in range(dp):
            out_ref[s, at : at + lines, :] = part[s * lines : (s + 1) * lines]
    leave(1, hlines, base_mixer - hlines)
    vectors = sums_ref[...].astype(bf16)
    part = dot(second_ref[...], plow_ref[...], TN).astype(bf16)
    for s in range(dp):
        for a in range(width // emb):
            at = s * lines + a * piece
            out_ref[s, base_project : base_project + piece, a * emb : (a + 1) * emb] = part[at : at + piece]
        out_ref[s, base_vec : base_vec + 16, :] = vectors
    one = one_ref[...]
    per = local // lines
    for r in range(parts):
        part = dot(arrived[r][...], one, TN).astype(bf16)
        j = lax.rem(place + r, parts)
        for i in range(per):
            out_ref[j * per + i, base_mixer : base_mixer + lines, :] = part[i * lines : (i + 1) * lines]
    rest = base_vec + 16 - base_mixer
    leave(2, base_mixer, rest)
    for stage, (at, count) in enumerate(
        ((0, hlines), (hlines, base_mixer - hlines), (base_mixer, rest))
    ):
        for s in range(dp):
            pltpu.make_async_copy(
                out_ref.at[s, pl.ds(at, count)], keep_ref.at[0, pl.ds(at, count)], sems.at[stage, s]
            ).wait()


def weight_grads(turn, place, arrived, first, active, second, plow, two, lifted, one, sums, dp):
    parts = len(arrived)
    tokens, width = first.shape
    hidden = active.shape[1]
    emb = plow.shape[1]
    lines, hlines = width // dp, hidden // dp
    total = hlines + lines * (hidden // width) + lines + lines * emb // width + 16
    V = pl.BlockSpec(memory_space=pltpu.VMEM)
    M = pl.BlockSpec(memory_space=pltpu.SMEM)
    return pl.pallas_call(
        functools.partial(weight_grads_kernel, parts, dp),
        out_shape=[jax.ShapeDtypeStruct((dp // 2, total, width), bf16)] * 2,
        in_specs=[M, M] + [V] * (parts + 8),
        out_specs=[pl.BlockSpec(memory_space=pl.ANY)] * 2,
        scratch_shapes=[pltpu.VMEM((dp, total, width), bf16), pltpu.SemaphoreType.DMA((3, dp))],
        compiler_params=pltpu.CompilerParams(vmem_limit_bytes=56 << 20),
        cost_estimate=SHORT,
        name="weight_grads",
    )(turn, place, *arrived, first, active, second, plow, two, lifted, one, sums)


def triple_grads_kernel(parts, heads, dp, turn_ref, *refs):
    blocks = refs[:parts]
    backs = refs[parts : parts + heads * parts]
    keep_ref, give_ref = refs[parts + heads * parts :]
    width = blocks[0].shape[1]
    lines = width // dp
    turn = turn_ref[0]
    ones = jnp.ones((16, blocks[0].shape[0]), bf16)
    total = sums = None
    for r in range(parts):
        grad = jnp.concatenate([backs[h * parts + r][...] for h in range(heads)], axis=1)
        part, line = dot(blocks[r][...], grad, TN), dot(ones, grad, NN)
        total = part if r == 0 else total + part
        sums = line if r == 0 else sums + line
    total, sums = total.astype(bf16), sums.astype(bf16)
    columns = slice(0, total.shape[1])
    for s in range(dp):
        k = lax.bitwise_xor(turn, s)
        put(keep_ref, give_ref, k, slice(0, lines), columns, total[s * lines : (s + 1) * lines])
        put(keep_ref, give_ref, k, slice(lines, lines + 16), columns, sums)


def triple_grads(turn, blocks, backs, dp):
    parts, heads = len(blocks), len(backs)
    count, width = blocks[0].shape
    V = pl.BlockSpec(memory_space=pltpu.VMEM)
    return pl.pallas_call(
        functools.partial(triple_grads_kernel, parts, heads, dp),
        out_shape=[jax.ShapeDtypeStruct((dp // 2, width // dp + 16, 3 * HD * heads), bf16)] * 2,
        in_specs=[pl.BlockSpec(memory_space=pltpu.SMEM)] + [V] * (parts + heads * parts),
        out_specs=[V] * 2,
        compiler_params=pltpu.CompilerParams(vmem_limit_bytes=56 << 20),
        cost_estimate=SHORT,
        name="triple_grads",
    )(turn, *blocks, *[b for back in backs for b in back])


FOUR = (0, 2, 1, 3)


def unpack_kernel(slabs, place_ref, turn_ref, near_ref, far_ref, *refs):
    outs, all_ref = refs[:-1], refs[-1]
    shrink_ref, expand_ref, mixer_ref, project_ref = outs[:4]
    count, width = near_ref.shape[1:]
    for i, k in enumerate(FOUR):
        j = lax.bitwise_xor(place_ref[0], k)
        piece = (near_ref, far_ref)[i // 2][i % 2]
        all_ref[pl.ds(pl.multiple_of(j * count, count), count), :] = piece.astype(f32)
    lines, emb = project_ref.shape
    at = shrink_ref.shape[0]
    shrink_ref[...] = all_ref[:at, :]
    for c in range(slabs):
        expand_ref[:, c * width : (c + 1) * width] = all_ref[at : at + lines, :]
        at += lines
    mixer_ref[...] = all_ref[at : at + lines, :]
    at += lines
    piece = lines * emb // width
    for a in range(width // emb):
        project_ref[a * piece : (a + 1) * piece, :] = all_ref[at : at + piece, a * emb : (a + 1) * emb]
    at += piece
    mine = turn_ref[0]
    turned = pltpu.roll(all_ref[at : at + 8, :], width - mine * lines, 1)
    for i in range(6):
        outs[4 + i][...] = turned[i, :lines]
    hlines = outs[10].shape[0]
    per = width // hlines
    line = all_ref[pl.ds(at + 6 + lax.div(mine, per), 1), :]
    line = jnp.broadcast_to(line, (8, width))
    outs[10][...] = pltpu.roll(line, width - lax.rem(mine, per) * hlines, 1)[0, :hlines]


def unpack(place, turn, pairs, dp, hidden, emb):
    count, width = pairs[0].shape[1:]
    lines, hlines = width // dp, hidden // dp
    S = jax.ShapeDtypeStruct
    V = pl.BlockSpec(memory_space=pltpu.VMEM)
    M = pl.BlockSpec(memory_space=pltpu.SMEM)
    return pl.pallas_call(
        functools.partial(unpack_kernel, hidden // width),
        out_shape=[
            S((hlines, width), f32),
            S((lines, hidden), f32),
            S((lines, width), f32),
            S((lines, emb), f32),
        ]
        + [S((lines,), f32)] * 6
        + [S((hlines,), f32)],
        in_specs=[M, M, V, V],
        out_specs=[V] * 11,
        scratch_shapes=[pltpu.VMEM((4 * count, width), f32)],
        cost_estimate=SHORT,
        name="unpack",
    )(place, turn, *pairs)


def unpack_triple_kernel(heads, place_ref, turn_ref, *refs):
    four, (triple_ref, queries_ref, values_ref, all_ref) = refs[:-4], refs[-4:]
    parts = len(four)
    lines = triple_ref.shape[0]
    local = heads * HD
    width = parts * local
    for piece, k in zip(four, FOUR):
        all_ref[lax.bitwise_xor(place_ref[0], k)] = piece[...].astype(f32)
    for kind in range(3):
        part = jnp.concatenate(
            [
                all_ref[j][: lines + 8, (3 * h + kind) * HD : (3 * h + kind + 1) * HD]
                for j in range(parts)
                for h in range(heads)
            ],
            axis=1,
        )
        triple_ref[:, kind * width : (kind + 1) * width] = part[:lines]
        if kind != 1:
            sums = pltpu.roll(part[lines:], width - turn_ref[0] * lines, 1)
            (queries_ref, None, values_ref)[kind][...] = sums[0, :lines]


def unpack_triple(place, turn, four, heads):
    parts = len(four)
    count, columns = four[0].shape
    lines = count - 16
    S = jax.ShapeDtypeStruct
    V = pl.BlockSpec(memory_space=pltpu.VMEM)
    M = pl.BlockSpec(memory_space=pltpu.SMEM)
    return pl.pallas_call(
        functools.partial(unpack_triple_kernel, heads),
        out_shape=[S((lines, parts * columns), f32), S((lines,), f32), S((lines,), f32)],
        in_specs=[M, M] + [V] * parts,
        out_specs=[V] * 3,
        scratch_shapes=[pltpu.VMEM((parts, count, columns), f32)],
        cost_estimate=SHORT,
        name="unpack_triple",
    )(place, turn, *four)


def gather(v):
    return lax.all_gather(v, "dp", axis=0, tiled=False)


def send(v, shift):
    if shift == 0:
        return v
    parts = lax.axis_size("seq")
    return lax.ppermute(v, "seq", [(i, (i + shift) % parts) for i in range(parts)])


def hop(v, step):
    parts = lax.axis_size("seq")
    return lax.ppermute(v, "seq", [(i, i + step) for i in range(parts) if 0 <= i + step < parts])


def swap(v, bits):
    return lax.ppermute(v, "dp", [(i, i ^ bits) for i in range(lax.axis_size("dp"))])


def double(v, bits):
    return jnp.concatenate([v, swap(v, bits)])


def together(*values):
    return lax.optimization_barrier(values)


def add(a, b):
    return (a.astype(f32) + b.astype(f32)).astype(bf16)


def sum_dp_core(keep, other):
    half = keep.shape[1] // 32 * 16
    a, b = slice(0, half), slice(half, None)
    pick = lambda rows, *slots: jnp.concatenate(
        [add(keep[i : i + 1, rows], other[i : i + 1, rows]) for i in slots]
    )
    return (pick(a, 0, 1), pick(a, 2, 3), pick(b, 0, 2), pick(b, 1, 3))


def sum_dp_first(sums):
    a_keep, a_give, b_keep, b_give = sums
    return (a_keep, swap(a_give, 2), b_keep, swap(b_give, 4))


def sum_dp_second(sums):
    a_keep, a_came, b_keep, b_came = sums
    a, b = add(a_keep, a_came), add(b_keep, b_came)
    return (a[0], a[1], b[0], b[1])


def sum_dp_last(sums):
    a_keep, a_give, b_keep, b_give = sums
    return (a_keep, swap(a_give, 4), b_keep, swap(b_give, 2))


def swap_seq(v, bits):
    return lax.ppermute(v, "seq", [(i, i ^ bits) for i in range(lax.axis_size("seq"))])


def turned_seq(items):
    place = lax.axis_index("seq")
    came = jnp.stack(items)
    return [
        lax.dynamic_index_in_dim(came, lax.bitwise_xor(place, k), keepdims=False)
        for k in range(len(items))
    ]


def sum_seq_first(v):
    v = v.reshape(4, -1, v.shape[1])
    v = turned_seq([v[i] for i in range(4)])
    came = swap_seq(jnp.stack([v[1], v[3]]), 1)
    return add(v[0], came[0]), add(v[2], came[1])


def sum_seq_second(v):
    return add(v[0], swap_seq(v[1], 2))


def rows_of(pieces, dp, width):
    flat = jnp.concatenate(pieces, axis=1)
    pad = -flat.shape[1] % width
    return jnp.pad(flat, ((0, 0), (0, pad))).reshape(dp, -1, width)


def shards(
    layer_input,
    triple_weight,
    query_bias,
    value_bias,
    mixer_weight,
    mixer_bias,
    first_gain,
    first_shift,
    expand_weight,
    expand_bias,
    shrink_weight,
    shrink_bias,
    second_gain,
    second_shift,
    project_weight,
    kept_tokens,
    upstream,
):
    parts = lax.axis_size("seq")
    dp = lax.axis_size("dp")
    place = lax.axis_index("seq")
    mine = lax.axis_index("dp")
    rows = layer_input[0]
    tokens, width = rows.shape
    local = width // parts
    heads = local // HD
    lines = width // dp
    hidden = expand_weight.shape[1]
    hlines = hidden // dp
    emb = project_weight.shape[1]

    fast = dp == 8 and parts == 4 and heads == 3 and lines % 16 == 0
    if not fast:
        blocks = [send(rows, r) for r in range(parts)]

    where = jnp.reshape(place, (1,))
    turn = jnp.reshape(mine, (1,))
    vectors = [
        query_bias,
        value_bias,
        mixer_bias,
        first_gain,
        first_shift,
        shrink_bias,
        second_gain,
        second_shift,
        expand_bias,
    ]
    both = jnp.concatenate([mixer_weight, project_weight], axis=1)
    if fast:
        wide, shrink = jnp.concatenate([expand_weight, both], axis=1)[None], shrink_weight[None]
        own, rest = prepare(where, triple_weight, vectors, parts)
        x_first, y_first = [(0, 2), (4, 6), (1, 3), (5, 7)], [(0, 4), (2, 6), (1, 5), (3, 7)]
        below, above = [rows, hop(rows, 1)], [rows, hop(rows, -1)]
        own = [own] + [swap(own, k) for k in (2, 4, 6)]
        own, below[1], above[1], wide, shrink = lax.optimization_barrier(
            (own, below[1], above[1], wide, shrink)
        )
        below.append(hop(below[1], 1))
        above.append(hop(above[1], -1))
        own = jnp.stack(own)
        own = [own, swap(own, 1)]
        wide, shrink = double(wide, 2), double(shrink, 4)
        below[2], above[2], wide, shrink, own = lax.optimization_barrier(
            (below[2], above[2], wide, shrink, own)
        )
        below.append(hop(below[2], 1))
        above.append(hop(above[2], -1))
        w_wide = [wide, swap(wide, 4)]
        w_shrink = [shrink, swap(shrink, 2)]
        w_own, bias, vec, b_expand = assemble(
            where, turn, own, [(0, 2, 4, 6), (1, 3, 5, 7)], parts, dp, hidden
        )
        blocks = [rows] + [
            jnp.where(place >= r, below[r], above[parts - r]) for r in range(1, parts)
        ]
    else:
        turned = jnp.roll(
            triple_weight.reshape(lines, 3, parts, heads, HD), -place, axis=2
        ).transpose(0, 2, 3, 1, 4)
        w_own = gather(turned[:, 0].reshape(lines, 3 * local)).reshape(width, 3 * local)
        w_rest = [gather(turned[:, 1:].swapaxes(1, 2).reshape(lines, -1)).reshape(1, width, -1)]
        small = gather(jnp.concatenate(vectors)).astype(f32)
        vec = jnp.stack([small[:, i * lines : (i + 1) * lines].reshape(width) for i in range(8)])
        b_expand = small[:, 8 * lines :].reshape(1, hidden)
        b_query, b_value = [
            lax.dynamic_slice(vec[i], (place * local,), (local,)).reshape(heads, HD) for i in (0, 1)
        ]
        bias = jnp.stack([b_query, jnp.zeros((heads, HD), f32), b_value], axis=1).reshape(1, -1)
        w_wide = [gather(jnp.concatenate([expand_weight, both], axis=1)).reshape(1, width, -1)]
        w_shrink = [gather(shrink_weight).reshape(1, hidden, width)]
        x_first = y_first = [(0,)]

    joined = [(dot(b, w_own, NN) + bias).astype(bf16) for b in blocks]
    order = list(range(2, parts)) + [1, 0]
    mixed_own = [None] * parts
    stats = [None] * parts
    arrived = [None] * parts
    for i, r in enumerate(order):
        if i > 0:
            joined, mixed_own[order[i - 1]] = together(joined, mixed_own[order[i - 1]])
        if fast and i == 0:
            early = [swap(w_wide[0], 1), swap(w_shrink[0], 1)]
            joined, early = together(joined, early)
        mixed_own[r], stats[r] = attend_forward(joined, r, heads)
        arrived[r] = send(mixed_own[r], -r)
    if fast:
        w_wide[1], w_shrink[1], mixed_own[0], arrived[2], arrived[3] = lax.optimization_barrier(
            (w_wide[1], w_shrink[1], mixed_own[0], arrived[2], arrived[3])
        )
        w_wide += [early[0], swap(w_wide[1], 1)]
        w_shrink += [early[1], swap(w_shrink[1], 1)]
        rest, arrived, w_wide[3], w_shrink[3] = together(rest[None], arrived, w_wide[3], w_shrink[3])
        rest = double(rest, 2)
    results = feed_forward(
        where,
        turn,
        rows,
        arrived,
        vec,
        b_expand,
        kept_tokens[0].astype(f32)[:, None],
        upstream[0],
        w_wide,
        x_first,
        w_shrink,
        y_first,
    )
    embedded, grad_resid_one, first, active, second, plow, two, lifted, one, sums = results[:10]
    grads = [send(g, r) for r, g in enumerate(results[10:])]

    slabs = hidden // width
    backs = []
    landed = []
    inputs = (joined, grads, mixed_own, stats)

    def backward(h, inputs):
        back = attend_backward(*inputs, h)
        backs.append(back)
        landed.append([send(back[r], -r) for r in range(parts)])

    if fast:
        first, rest = together(first, rest)
        w_rest = [rest, swap(rest, 4)]
        keep, give = weight_grads(
            turn, where, arrived, first, active, second, plow, two, lifted, one, sums, dp
        )
        grads, give, w_rest = together(grads, give, w_rest)
        other = swap(give, 1)
        w_rest += [swap(w, 1) for w in w_rest]
        inputs, keep = together((joined, grads, mixed_own, stats), keep)
        backward(0, inputs)
        keep, other, backs[0] = together(keep, other, backs[0])
        batch = sum_dp_core(keep, other)
        inputs, batch, w_rest = together(inputs, batch, w_rest)
        batch = sum_dp_first(batch)
        backward(1, inputs)
        batch, landed[0], backs[1] = together(batch, landed[0], backs[1])
        batch = sum_dp_second(batch)
        inputs, batch = together(inputs, batch)
        batch = sum_dp_last(batch)
        backward(2, inputs)
        batch = jnp.concatenate([add(batch[0], batch[1]), add(batch[2], batch[3])])
        backs, landed[1], batch = together(backs, landed[1], batch)
        batch = sum_seq_first(batch)
        keep, give = triple_grads(turn, blocks, backs, dp)
        give, batch, landed[2] = together(give, batch, landed[2])
        last = add(keep, swap(give, 1))
        last = add(last[:2], swap(last[2:], 2))
        last = add(last[0], swap(last[1], 4))
        batch = sum_seq_second(batch)
        input_grad = input_gradient(turn, grad_resid_one, w_own, landed, w_rest, x_first)
        batch, last, input_grad = together(batch, last, input_grad)
        last = [last, swap_seq(last, 2)]
        both = jnp.stack([batch, swap_seq(batch, 2)])
        both, last = together(both, last)
        last += [swap_seq(v, 1) for v in last]
        r_triple, r_queries, r_values = unpack_triple(where, turn, last, heads)
        outs = unpack(where, turn, [both, swap_seq(both, 1)], dp, hidden, emb)
        r_shrink, r_expand, r_mixer, r_project = outs[:4]
        r_offset, r_gamma, r_beta, r_settle, r_gain, r_shift, r_lift = outs[4:]
    else:
        g_expand = dot(first, lifted, TN).astype(bf16)
        mixed = jnp.concatenate(arrived, axis=1)
        g_mixer = jnp.roll(dot(mixed, one, TN).reshape(parts, local, width), place, axis=0)
        g_project = dot(second, plow, TN).astype(bf16)
        batch = jnp.concatenate(
            [
                dot(active, two, TN).astype(bf16).reshape(dp, hlines, width),
                *[
                    g_expand[:, c * width : (c + 1) * width].reshape(dp, lines, width)
                    for c in range(slabs)
                ],
                g_mixer.astype(bf16).reshape(dp, lines, width),
                jnp.stack([rows_of([g[None].reshape(1, -1)], 1, width)[0] for g in g_project.reshape(dp, lines, emb)]),
                jnp.broadcast_to(sums.astype(bf16), (dp,) + sums.shape),
            ],
            axis=1,
        )
        batch = lax.psum_scatter(batch, "dp", scatter_dimension=0, tiled=False)
        batch = lax.psum(batch, "seq")
        for h in range(heads):
            backward(h, inputs)
        g_own = jnp.concatenate([jnp.concatenate(back, axis=0) for back in backs], axis=1)
        g_triple = dot(jnp.concatenate(blocks, axis=0), g_own, TN)
        columns = jnp.sum(g_own.astype(f32), axis=0).astype(bf16)
        last = jnp.concatenate(
            [
                g_triple.astype(bf16).reshape(dp, lines, 3 * local),
                jnp.broadcast_to(columns, (dp, 1, 3 * local)),
            ],
            axis=1,
        )
        last = lax.psum_scatter(last, "dp", scatter_dimension=0, tiled=False)
        last = lax.all_gather(last, "seq", axis=0, tiled=False)
        batch = batch.astype(f32)
        r_shrink = batch[:hlines]
        at = hlines
        r_expand = jnp.concatenate(
            [batch[at + c * lines : at + (c + 1) * lines] for c in range(slabs)], axis=1
        )
        at += lines * slabs
        r_mixer = batch[at : at + lines]
        at += lines
        piece = lines * emb // width
        r_project = batch[at : at + piece].reshape(lines, emb)
        tail = batch[at + piece :]
        r_offset, r_gamma, r_beta, r_settle, r_gain, r_shift = [
            lax.dynamic_slice(tail[i], (mine * lines,), (lines,)) for i in range(6)
        ]
        r_lift = lax.dynamic_slice(
            tail[6 : 6 + slabs].reshape(hidden), (mine * hlines,), (hlines,)
        )

        last = last.astype(f32)
        last = last.reshape(parts, lines + 1, heads, 3, HD).transpose(1, 3, 0, 2, 4)
        r_triple = last[:lines].reshape(lines, 3 * width)
        sums = last[lines].reshape(3, width)
        r_queries = lax.dynamic_slice(sums[0], (mine * lines,), (lines,))
        r_values = lax.dynamic_slice(sums[2], (mine * lines,), (lines,))
        input_grad = input_gradient(turn, grad_resid_one, w_own, landed, w_rest, x_first)
    return (
        embedded[None],
        input_grad[None],
        r_triple,
        r_queries,
        r_values,
        r_mixer,
        r_offset,
        r_gamma,
        r_beta,
        r_expand,
        r_lift,
        r_shrink,
        r_settle,
        r_gain,
        r_shift,
        r_project,
    )


def solution(mesh):
    whole = P("dp", "seq", None)
    rows = P("dp", None)
    flat = P("dp")
    in_specs = (
        whole,
        rows,
        flat,
        flat,
        rows,
        flat,
        flat,
        flat,
        rows,
        flat,
        rows,
        flat,
        flat,
        flat,
        rows,
        P("dp", "seq"),
        whole,
    )
    out_specs = (
        whole,
        whole,
        rows,
        flat,
        flat,
        rows,
        flat,
        flat,
        flat,
        rows,
        flat,
        rows,
        flat,
        flat,
        flat,
        rows,
    )
    return jax.shard_map(shards, mesh=mesh, in_specs=in_specs, out_specs=out_specs, check_vma=False)
```

```python
import functools

import jax
import jax.numpy as jnp
from jax import lax
from jax.experimental import pallas as pl
from jax.experimental.pallas import tpu as pltpu
from jax.sharding import PartitionSpec as P

HD = 64
LOG2E = 1.4426950408889634
f32 = jnp.float32
bf16 = jnp.bfloat16
SHORT = pl.CostEstimate(flops=0, transcendentals=0, bytes_accessed=0)
NT = (((1,), (1,)), ((), ()))
NN = (((1,), (0,)), ((), ()))
TN = (((0,), (0,)), ((), ()))


def dot(a, b, dims):
    return lax.dot_general(a, b, dims, preferred_element_type=f32)


def attend_forward_kernel(parts, block, heads, *refs):
    joined = refs[:parts]
    mixed_ref, stats_ref = refs[parts:]
    count = joined[0].shape[0]
    for h in range(heads):
        base = 3 * HD * h
        query = joined[block][:, base : base + HD] * jnp.asarray(HD**-0.5, bf16)
        scores = [
            dot(query, j[:, base + HD : base + 2 * HD], NT) * LOG2E for j in joined
        ]
        top = jnp.max(scores[0], axis=1, keepdims=True)
        for s in scores[1:]:
            top = jnp.maximum(top, jnp.max(s, axis=1, keepdims=True))
        total = None
        for s, j in zip(scores, joined):
            probs = jnp.exp2(s - top).astype(bf16)
            wide = jnp.concatenate(
                [j[:, base + 2 * HD : base + 3 * HD], jnp.ones((count, HD), bf16)], axis=1
            )
            part = dot(probs, wide, NN)
            total = part if total is None else total + part
        mass = total[:, HD : HD + 1]
        mixed_ref[:, HD * h : HD * (h + 1)] = (total[:, :HD] / mass).astype(bf16)
        stats_ref[:, h : h + 1] = top + jnp.log2(mass)


def attend_forward(joined, block, heads):
    parts = len(joined)
    count = joined[0].shape[0]
    return pl.pallas_call(
        functools.partial(attend_forward_kernel, parts, block, heads),
        out_shape=[
            jax.ShapeDtypeStruct((count, heads * HD), bf16),
            jax.ShapeDtypeStruct((count, 8), f32),
        ],
        in_specs=[pl.BlockSpec(memory_space=pltpu.VMEM)] * parts,
        out_specs=[pl.BlockSpec(memory_space=pltpu.VMEM)] * 2,
        compiler_params=pltpu.CompilerParams(vmem_limit_bytes=40 << 20),
        cost_estimate=SHORT,
        name="attend_forward",
    )(*joined)


def attend_backward_kernel(parts, h, *refs):
    joined = refs[:parts]
    grads = refs[parts : 2 * parts]
    mixed = refs[2 * parts : 3 * parts]
    stats = refs[3 * parts : 4 * parts]
    outs = refs[4 * parts : 5 * parts]
    keys_sum, values_sum = refs[5 * parts :]
    base = 3 * HD * h
    count = joined[0].shape[0]
    for b in range(parts):
        query = joined[b][:, base : base + HD] * jnp.asarray(HD**-0.5, bf16)
        grad = grads[b][:, HD * h : HD * (h + 1)]
        inner = jnp.sum(
            grad.astype(f32) * mixed[b][:, HD * h : HD * (h + 1)].astype(f32), axis=1, keepdims=True
        )
        level = stats[b][:, h : h + 1]
        query_t = query.T
        grad_t = grad.T
        total = None
        for c in range(parts):
            keys = joined[c][:, base + HD : base + 2 * HD]
            values = joined[c][:, base + 2 * HD : base + 3 * HD]
            probs = jnp.exp2(dot(query, keys, NT) * LOG2E - level)
            grad_probs = dot(grad, values, NT)
            grad_scores = (probs * (grad_probs - inner)).astype(bf16)
            part = dot(grad_scores, keys, NN)
            total = part if total is None else total + part
            span = slice(c * count, (c + 1) * count)
            grad_values = dot(grad_t, probs.astype(bf16), NN)
            grad_keys = dot(query_t, grad_scores, NN)
            if b == 0:
                values_sum[:, span] = grad_values
                keys_sum[:, span] = grad_keys
            else:
                values_sum[:, span] += grad_values
                keys_sum[:, span] += grad_keys
        outs[b][:, :HD] = (total * HD**-0.5).astype(bf16)
    for c in range(parts):
        span = slice(c * count, (c + 1) * count)
        outs[c][:, HD : 2 * HD] = keys_sum[:, span].T.astype(bf16)
        outs[c][:, 2 * HD :] = values_sum[:, span].T.astype(bf16)


def attend_backward(joined, grads, mixed, stats, h):
    parts = len(joined)
    count = joined[0].shape[0]
    return pl.pallas_call(
        functools.partial(attend_backward_kernel, parts, h),
        out_shape=[jax.ShapeDtypeStruct((count, 3 * HD), bf16)] * parts,
        grid=(1,),
        scratch_shapes=[pltpu.VMEM((HD, parts * count), f32)] * 2,
        compiler_params=pltpu.CompilerParams(vmem_limit_bytes=60 << 20),
        cost_estimate=SHORT,
        name="attend_backward",
    )(*joined, *grads, *mixed, *stats)


def normal_cdf_and_density(x):
    a = jnp.abs(x) * (0.5**0.5)
    t = 1.0 / (1.0 + 0.5 * a)
    series = -0.82215223 + t * 0.17087277
    for c in (1.48851587, -1.13520398, 0.27886807, -0.18628806, 0.09678418, 0.37409196, 1.00002368):
        series = c + t * series
    tail = 0.5 * t * jnp.exp(-a * a - 1.26551223 + t * series)
    cdf = jnp.where(x >= 0, 1.0 - tail, tail)
    return cdf, jnp.exp(-0.5 * x * x) * 0.3989422804014327


def standardize(rows):
    mean = jnp.mean(rows, axis=-1, keepdims=True)
    centred = rows - mean
    spread = jnp.mean(centred * centred, axis=-1, keepdims=True)
    scale = lax.rsqrt(spread + 1e-12)
    return centred * scale, scale


def norm_back(grad, gain, normed, scale):
    g = grad * gain
    return (
        g
        - jnp.mean(g, axis=-1, keepdims=True)
        - normed * jnp.mean(g * normed, axis=-1, keepdims=True)
    ) * scale


def ffn_kernel(parts, step, wide_from, shrink_from, place_ref, turn_ref, *refs):
    rows_ref, arrived, refs = refs[0], refs[1 : 1 + parts], refs[1 + parts :]
    vec_ref, lift_bias_ref, keep_ref, ct_ref = refs[:4]
    groups = len(wide_from)
    wide_hbm, shrink_hbm = refs[4 : 4 + groups], refs[4 + groups : 4 + 2 * groups]
    outs = refs[4 + 2 * groups :]
    (embedded_ref, resid_ref, first_ref, active_ref, second_ref, plow_ref, two_ref, lifted_ref, one_ref, sums_ref) = outs[:10]
    mixed_grads = outs[10 : 10 + parts]
    mixer_ref, expand_ref, shrink_ref, slope_ref, total_ref, sems = outs[10 + parts :]
    width = rows_ref.shape[1]
    hidden = lift_bias_ref.shape[1]
    local = width // parts
    chunks = hidden // step
    place = place_ref[0]

    pieces = sum(len(f) for f in wide_from)

    def load(sources, origin, columns, target, first):
        count = target.shape[0] // pieces
        copies = []
        for source, ks in zip(sources, origin):
            for i, k in enumerate(ks):
                at = pl.multiple_of(lax.bitwise_xor(turn_ref[0], k) * count, count) if pieces > 1 else 0
                copies.append(
                    pltpu.make_async_copy(
                        source.at[i, :, columns],
                        target.at[pl.ds(at, count), :],
                        sems.at[first + len(copies)],
                    )
                )
                copies[-1].start()
        return copies

    side = width + ct_ref.shape[1]
    load_mixer = load(wide_hbm, wide_from, slice(hidden, hidden + side), mixer_ref, 0)
    load_expand = load(wide_hbm, wide_from, slice(0, hidden), expand_ref, pieces)
    load_shrink = load(shrink_hbm, shrink_from, slice(0, width), shrink_ref, 2 * pieces)

    def vec(i):
        return vec_ref[i : i + 1, :]

    def mixer_rows(r):
        at = lax.rem(place + r, parts) * local
        return mixer_ref[pl.ds(pl.multiple_of(at, local), local), :width]

    for copy in load_mixer:
        copy.wait()
    branch = vec(2)
    for r in range(parts):
        branch = branch + dot(arrived[r][...], mixer_rows(r), NN)
    normed_one, scale_one = standardize(rows_ref[...].astype(f32) + branch)
    first = normed_one * vec(3) + vec(4)
    first_low = first.astype(bf16)
    first_ref[...] = first_low
    total_ref[...] = first + vec(5)

    for copy in load_expand + load_shrink:
        copy.wait()

    def forward(c, carry):
        at = pl.multiple_of(c * step, step)
        lifted = dot(first_ref[...], expand_ref[:, pl.ds(at, step)], NN) + lift_bias_ref[:, pl.ds(at, step)]
        cdf, density = normal_cdf_and_density(lifted)
        active = (lifted * cdf).astype(bf16)
        active_ref[:, pl.ds(at, step)] = active
        slope_ref[:, pl.ds(at, step)] = cdf + lifted * density
        total_ref[...] += dot(active, shrink_ref[pl.ds(at, step), :], NN)
        return carry

    lax.fori_loop(0, chunks, forward, 0, unroll=True)

    normed_two, scale_two = standardize(total_ref[...])
    second_low = (normed_two * vec(6) + vec(7)).astype(bf16)
    second_ref[...] = second_low
    w_project = mixer_ref[:, width:]
    projected = dot(second_low, w_project, NN)
    keep = keep_ref[...]
    inverse = lax.rsqrt(jnp.sum(projected * projected, axis=-1, keepdims=True) + 1e-06)
    unit = projected * inverse
    embedded_ref[...] = unit * keep
    ct = ct_ref[...]
    plow = (keep * (ct - unit * jnp.sum(unit * ct, axis=-1, keepdims=True)) * inverse).astype(bf16)
    plow_ref[...] = plow
    grad_second = dot(plow, w_project, NT)
    sums_ref[4:5, :] = jnp.sum(grad_second * normed_two, axis=0, keepdims=True)
    sums_ref[5:6, :] = jnp.sum(grad_second, axis=0, keepdims=True)
    grad_two = norm_back(grad_second, vec(6), normed_two, scale_two)
    two_low = grad_two.astype(bf16)
    two_ref[...] = two_low
    sums_ref[3:4, :] = jnp.sum(two_low.astype(f32), axis=0, keepdims=True)
    total_ref[...] = grad_two

    def backward(c, carry):
        at = pl.multiple_of(c * step, step)
        grad_active = dot(two_ref[...], shrink_ref[pl.ds(at, step), :], NT)
        low = (grad_active * slope_ref[:, pl.ds(at, step)]).astype(bf16)
        lifted_ref[:, pl.ds(at, step)] = low
        total_ref[...] += dot(low, expand_ref[:, pl.ds(at, step)], NT)
        return carry

    lax.fori_loop(0, chunks, backward, 0, unroll=True)
    for c in range(hidden // width):
        sums_ref[6 + c : 7 + c, :] = jnp.sum(
            lifted_ref[:, c * width : (c + 1) * width].astype(f32), axis=0, keepdims=True
        )

    grad_first = total_ref[...]
    sums_ref[1:2, :] = jnp.sum(grad_first * normed_one, axis=0, keepdims=True)
    sums_ref[2:3, :] = jnp.sum(grad_first, axis=0, keepdims=True)
    grad_one = norm_back(grad_first, vec(3), normed_one, scale_one)
    resid_ref[...] = grad_one
    one_low = grad_one.astype(bf16)
    one_ref[...] = one_low
    sums_ref[0:1, :] = jnp.sum(one_low.astype(f32), axis=0, keepdims=True)
    for r in range(parts):
        mixed_grads[r][...] = dot(one_low, mixer_rows(r), NT).astype(bf16)
    used = 6 + hidden // width
    sums_ref[used:, :] = jnp.zeros((sums_ref.shape[0] - used, width), f32)


def feed_forward(place, turn, rows, arrived, vec, lift_bias, keep, ct, wide, wide_from, shrink, shrink_from):
    parts = len(arrived)
    groups = len(wide)
    pieces = sum(len(f) for f in wide_from)
    tokens, width = rows.shape
    hidden = lift_bias.shape[1]
    emb = ct.shape[1]
    local = width // parts
    V = pl.BlockSpec(memory_space=pltpu.VMEM)
    A = pl.BlockSpec(memory_space=pl.ANY)
    M = pl.BlockSpec(memory_space=pltpu.SMEM)
    S = jax.ShapeDtypeStruct
    return pl.pallas_call(
        functools.partial(ffn_kernel, parts, hidden // 4, wide_from, shrink_from),
        out_shape=[
            S((tokens, emb), f32),
            S((tokens, width), f32),
            S((tokens, width), bf16),
            S((tokens, hidden), bf16),
            S((tokens, width), bf16),
            S((tokens, emb), bf16),
            S((tokens, width), bf16),
            S((tokens, hidden), bf16),
            S((tokens, width), bf16),
            S((16, width), f32),
        ]
        + [S((tokens, local), bf16)] * parts,
        in_specs=[M, M, V] + [V] * parts + [V] * 4 + [A] * (2 * groups),
        out_specs=[V] * (10 + parts),
        scratch_shapes=[
            pltpu.VMEM((width, width + emb), bf16),
            pltpu.VMEM((width, hidden), bf16),
            pltpu.VMEM((hidden, width), bf16),
            pltpu.VMEM((tokens, hidden), f32),
            pltpu.VMEM((tokens, width), f32),
            pltpu.SemaphoreType.DMA((3 * pieces,)),
        ],
        compiler_params=pltpu.CompilerParams(vmem_limit_bytes=56 << 20),
        cost_estimate=SHORT,
        name="feed_forward",
    )(place, turn, rows, *arrived, vec, lift_bias, keep, ct, *wide, *shrink)


def prepare_kernel(parts, heads, place_ref, triple_ref, *refs):
    vectors, (own_ref, rest_ref) = refs[:-2], refs[-2:]
    lines = triple_ref.shape[0]
    local = heads * HD
    width = parts * local
    shift = lax.rem(parts - place_ref[0], parts) * local
    kinds = [
        pltpu.roll(triple_ref[:, i * width : (i + 1) * width].astype(f32), shift, 1).astype(bf16)
        for i in range(3)
    ]
    for h in range(heads):
        for r in range(parts):
            piece = jnp.concatenate(
                [k[:, r * local + h * HD : r * local + (h + 1) * HD] for k in kinds], axis=1
            )
            if r == 0:
                own_ref[:lines, h * 3 * HD : (h + 1) * 3 * HD] = piece
            else:
                at = (h * (parts - 1) + r - 1) * 3 * HD
                rest_ref[:, at : at + 3 * HD] = piece
    lane = own_ref.shape[1]
    lined = [jnp.zeros((16 - len(vectors), lane), f32)]
    for v in vectors[::-1]:
        line = v[...].astype(f32).reshape(1, -1)
        lined.insert(0, jnp.pad(line, ((0, 0), (0, lane - line.shape[1]))))
    own_ref[lines:, :] = jnp.concatenate(lined).astype(bf16)


def prepare(place, triple, vectors, parts):
    lines, columns = triple.shape
    own = columns // parts
    V = pl.BlockSpec(memory_space=pltpu.VMEM)
    return pl.pallas_call(
        functools.partial(prepare_kernel, parts, own // (3 * HD)),
        out_shape=[
            jax.ShapeDtypeStruct((lines + 16, own), bf16),
            jax.ShapeDtypeStruct((lines, columns - own), bf16),
        ],
        in_specs=[pl.BlockSpec(memory_space=pltpu.SMEM), V] + [V] * len(vectors),
        out_specs=[V] * 2,
        cost_estimate=SHORT,
        name="prepare",
    )(place, triple, *vectors)


def assemble_kernel(parts, origin, place_ref, turn_ref, *refs):
    stacks, (w_ref, bias_ref, vec_ref, lift_ref, all_ref) = refs[:-5], refs[-5:]
    dp = all_ref.shape[0]
    lines = w_ref.shape[0] // dp
    hlines = lift_ref.shape[1] // dp
    width = vec_ref.shape[1]
    local = width // parts
    for stack, ks in zip(stacks, origin):
        for i, k in enumerate(ks):
            s = lax.bitwise_xor(turn_ref[0], k)
            w_ref[pl.ds(pl.multiple_of(s * lines, lines), lines), :] = stack[i, :lines, :]
            all_ref[s] = stack[i, lines:, :].astype(f32)
    vec_ref[...] = jnp.concatenate([all_ref[s][:8, :lines] for s in range(dp)], axis=1)
    lift_ref[...] = jnp.concatenate([all_ref[s][8:9, :hlines] for s in range(dp)], axis=1)
    shift = lax.rem(parts - place_ref[0], parts) * local
    turned = pltpu.roll(vec_ref[...], shift, 1)
    pieces = []
    for at in range(0, local, HD):
        pieces += [turned[0:1, at : at + HD], jnp.zeros((1, HD), f32), turned[1:2, at : at + HD]]
    bias_ref[...] = jnp.concatenate(pieces, axis=1)


def assemble(place, turn, stacks, origin, parts, dp, hidden):
    count, own = stacks[0].shape[1:]
    width = (count - 16) * dp
    V = pl.BlockSpec(memory_space=pltpu.VMEM)
    M = pl.BlockSpec(memory_space=pltpu.SMEM)
    return pl.pallas_call(
        functools.partial(assemble_kernel, parts, origin),
        out_shape=[
            jax.ShapeDtypeStruct((width, own), bf16),
            jax.ShapeDtypeStruct((1, own), f32),
            jax.ShapeDtypeStruct((8, width), f32),
            jax.ShapeDtypeStruct((1, hidden), f32),
        ],
        in_specs=[M, M] + [V] * len(stacks),
        out_specs=[V] * 4,
        scratch_shapes=[pltpu.VMEM((dp, 16, own), f32)],
        cost_estimate=SHORT,
        name="assemble",
    )(place, turn, *stacks)


def input_grad_kernel(origin, parts, heads, turn_ref, resid_ref, own_ref, *refs):
    landed, refs = refs[: heads * parts], refs[heads * parts :]
    stacks, (out_ref, rest_ref) = refs[: len(origin)], refs[len(origin) :]
    pieces = sum(len(ks) for ks in origin)
    count = rest_ref.shape[0] // pieces
    for source, ks in zip(stacks, origin):
        for i, k in enumerate(ks):
            at = pl.multiple_of(lax.bitwise_xor(turn_ref[0], k) * count, count) if pieces > 1 else 0
            rest_ref[pl.ds(at, count), :] = source[i]
    near = jnp.concatenate([landed[h * parts][...] for h in range(heads)], axis=1)
    far = jnp.concatenate(
        [landed[h * parts + r][...] for h in range(heads) for r in range(1, parts)], axis=1
    )
    out_ref[...] = resid_ref[...] + dot(near, own_ref[...], NT) + dot(far, rest_ref[...], NT)


def input_gradient(turn, resid, w_own, landed, stacks, origin):
    heads, parts = len(landed), len(landed[0])
    W = pl.BlockSpec()
    return pl.pallas_call(
        functools.partial(input_grad_kernel, origin, parts, heads),
        grid=(1,),
        out_shape=jax.ShapeDtypeStruct(resid.shape, f32),
        in_specs=[pl.BlockSpec(memory_space=pltpu.SMEM)] + [W] * (2 + heads * parts + len(stacks)),
        out_specs=W,
        scratch_shapes=[pltpu.VMEM((resid.shape[1], stacks[0].shape[2]), bf16)],
        compiler_params=pltpu.CompilerParams(vmem_limit_bytes=60 << 20),
        cost_estimate=SHORT,
        name="input_gradient",
    )(turn, resid, w_own, *[v for h in landed for v in h], *stacks)


def put(keep_ref, give_ref, k, rows, columns, value):
    place = 2 * lax.bitwise_and(lax.shift_right_logical(k, 1), 1) + lax.shift_right_logical(k, 2)

    @pl.when(lax.bitwise_and(k, 1) == 0)
    def _():
        keep_ref[place, rows, columns] = value

    @pl.when(lax.bitwise_and(k, 1) == 1)
    def _():
        give_ref[place, rows, columns] = value


def weight_grads_kernel(parts, dp, turn_ref, place_ref, *refs):
    arrived = refs[:parts]
    first_ref, active_ref, second_ref, plow_ref, two_ref, lifted_ref, one_ref, sums_ref = refs[parts : parts + 8]
    keep_ref, give_ref, out_ref, sems = refs[parts + 8 :]
    width = first_ref.shape[1]
    hidden = active_ref.shape[1]
    emb = plow_ref.shape[1]
    lines, hlines, local = width // dp, hidden // dp, width // parts
    turn = turn_ref[0]
    place = place_ref[0]
    slabs = hidden // width
    base_mixer = hlines + lines * slabs
    base_project = base_mixer + lines
    piece = lines * emb // width
    base_vec = base_project + piece

    def leave(stage, at, count):
        for s in range(dp):
            k = lax.bitwise_xor(turn, s)
            slot = 2 * lax.bitwise_and(lax.shift_right_logical(k, 1), 1) + lax.shift_right_logical(k, 2)
            source = out_ref.at[s, pl.ds(at, count)]
            sem = sems.at[stage, s]

            @pl.when(lax.bitwise_and(k, 1) == 0)
            def _():
                pltpu.make_async_copy(source, keep_ref.at[slot, pl.ds(at, count)], sem).start()

            @pl.when(lax.bitwise_and(k, 1) == 1)
            def _():
                pltpu.make_async_copy(source, give_ref.at[slot, pl.ds(at, count)], sem).start()

    two = two_ref[...]
    per = width // hlines
    for c in range(slabs):
        part = dot(active_ref[:, c * width : (c + 1) * width], two, TN).astype(bf16)
        for i in range(per):
            out_ref[c * per + i, :hlines, :] = part[i * hlines : (i + 1) * hlines]
    leave(0, 0, hlines)
    first = first_ref[...]
    for c in range(slabs):
        part = dot(first, lifted_ref[:, c * width : (c + 1) * width], TN).astype(bf16)
        at = hlines + c * lines
        for s in range(dp):
            out_ref[s, at : at + lines, :] = part[s * lines : (s + 1) * lines]
    leave(1, hlines, base_mixer - hlines)
    vectors = sums_ref[...].astype(bf16)
    part = dot(second_ref[...], plow_ref[...], TN).astype(bf16)
    for s in range(dp):
        for a in range(width // emb):
            at = s * lines + a * piece
            out_ref[s, base_project : base_project + piece, a * emb : (a + 1) * emb] = part[at : at + piece]
        out_ref[s, base_vec : base_vec + 16, :] = vectors
    one = one_ref[...]
    per = local // lines
    for r in range(parts):
        part = dot(arrived[r][...], one, TN).astype(bf16)
        j = lax.rem(place + r, parts)
        for i in range(per):
            out_ref[j * per + i, base_mixer : base_mixer + lines, :] = part[i * lines : (i + 1) * lines]
    rest = base_vec + 16 - base_mixer
    leave(2, base_mixer, rest)
    for stage, (at, count) in enumerate(
        ((0, hlines), (hlines, base_mixer - hlines), (base_mixer, rest))
    ):
        for s in range(dp):
            pltpu.make_async_copy(
                out_ref.at[s, pl.ds(at, count)], keep_ref.at[0, pl.ds(at, count)], sems.at[stage, s]
            ).wait()


def weight_grads(turn, place, arrived, first, active, second, plow, two, lifted, one, sums, dp):
    parts = len(arrived)
    tokens, width = first.shape
    hidden = active.shape[1]
    emb = plow.shape[1]
    lines, hlines = width // dp, hidden // dp
    total = hlines + lines * (hidden // width) + lines + lines * emb // width + 16
    V = pl.BlockSpec(memory_space=pltpu.VMEM)
    M = pl.BlockSpec(memory_space=pltpu.SMEM)
    return pl.pallas_call(
        functools.partial(weight_grads_kernel, parts, dp),
        out_shape=[jax.ShapeDtypeStruct((dp // 2, total, width), bf16)] * 2,
        in_specs=[M, M] + [V] * (parts + 8),
        out_specs=[pl.BlockSpec(memory_space=pl.ANY)] * 2,
        scratch_shapes=[pltpu.VMEM((dp, total, width), bf16), pltpu.SemaphoreType.DMA((3, dp))],
        compiler_params=pltpu.CompilerParams(vmem_limit_bytes=56 << 20),
        cost_estimate=SHORT,
        name="weight_grads",
    )(turn, place, *arrived, first, active, second, plow, two, lifted, one, sums)


def triple_grads_kernel(parts, heads, dp, turn_ref, *refs):
    blocks = refs[:parts]
    backs = refs[parts : parts + heads * parts]
    keep_ref, give_ref = refs[parts + heads * parts :]
    width = blocks[0].shape[1]
    lines = width // dp
    turn = turn_ref[0]
    ones = jnp.ones((16, blocks[0].shape[0]), bf16)
    total = sums = None
    for r in range(parts):
        grad = jnp.concatenate([backs[h * parts + r][...] for h in range(heads)], axis=1)
        part, line = dot(blocks[r][...], grad, TN), dot(ones, grad, NN)
        total = part if r == 0 else total + part
        sums = line if r == 0 else sums + line
    total, sums = total.astype(bf16), sums.astype(bf16)
    columns = slice(0, total.shape[1])
    for s in range(dp):
        k = lax.bitwise_xor(turn, s)
        put(keep_ref, give_ref, k, slice(0, lines), columns, total[s * lines : (s + 1) * lines])
        put(keep_ref, give_ref, k, slice(lines, lines + 16), columns, sums)


def triple_grads(turn, blocks, backs, dp):
    parts, heads = len(blocks), len(backs)
    count, width = blocks[0].shape
    V = pl.BlockSpec(memory_space=pltpu.VMEM)
    return pl.pallas_call(
        functools.partial(triple_grads_kernel, parts, heads, dp),
        out_shape=[jax.ShapeDtypeStruct((dp // 2, width // dp + 16, 3 * HD * heads), bf16)] * 2,
        in_specs=[pl.BlockSpec(memory_space=pltpu.SMEM)] + [V] * (parts + heads * parts),
        out_specs=[V] * 2,
        compiler_params=pltpu.CompilerParams(vmem_limit_bytes=56 << 20),
        cost_estimate=SHORT,
        name="triple_grads",
    )(turn, *blocks, *[b for back in backs for b in back])


FOUR = (0, 2, 1, 3)


def unpack_kernel(slabs, place_ref, turn_ref, *refs):
    pairs, outs, all_ref = refs[:4], refs[4:-1], refs[-1]
    shrink_ref, expand_ref, mixer_ref, project_ref = outs[:4]
    count, width = pairs[0].shape[1:]
    for half in range(2):
        for i, k in enumerate(FOUR):
            at = (4 * half + lax.bitwise_xor(place_ref[0], k)) * count
            piece = pairs[2 * half + i // 2][i % 2]
            all_ref[pl.ds(pl.multiple_of(at, count), count), :] = piece.astype(f32)
    lines, emb = project_ref.shape
    at = shrink_ref.shape[0]
    shrink_ref[...] = all_ref[:at, :]
    for c in range(slabs):
        expand_ref[:, c * width : (c + 1) * width] = all_ref[at : at + lines, :]
        at += lines
    mixer_ref[...] = all_ref[at : at + lines, :]
    at += lines
    piece = lines * emb // width
    for a in range(width // emb):
        project_ref[a * piece : (a + 1) * piece, :] = all_ref[at : at + piece, a * emb : (a + 1) * emb]
    at += piece
    mine = turn_ref[0]
    turned = pltpu.roll(all_ref[at : at + 8, :], width - mine * lines, 1)
    for i in range(6):
        outs[4 + i][...] = turned[i, :lines]
    hlines = outs[10].shape[0]
    per = width // hlines
    line = all_ref[pl.ds(at + 6 + lax.div(mine, per), 1), :]
    line = jnp.broadcast_to(line, (8, width))
    outs[10][...] = pltpu.roll(line, width - lax.rem(mine, per) * hlines, 1)[0, :hlines]


def unpack(place, turn, pairs, dp, hidden, emb):
    count, width = pairs[0].shape[1:]
    lines, hlines = width // dp, hidden // dp
    S = jax.ShapeDtypeStruct
    V = pl.BlockSpec(memory_space=pltpu.VMEM)
    M = pl.BlockSpec(memory_space=pltpu.SMEM)
    return pl.pallas_call(
        functools.partial(unpack_kernel, hidden // width),
        out_shape=[
            S((hlines, width), f32),
            S((lines, hidden), f32),
            S((lines, width), f32),
            S((lines, emb), f32),
        ]
        + [S((lines,), f32)] * 6
        + [S((hlines,), f32)],
        in_specs=[M, M] + [V] * 4,
        out_specs=[V] * 11,
        scratch_shapes=[pltpu.VMEM((8 * count, width), f32)],
        cost_estimate=SHORT,
        name="unpack",
    )(place, turn, *pairs)


def unpack_triple_kernel(heads, place_ref, turn_ref, *refs):
    four, (triple_ref, queries_ref, values_ref, all_ref) = refs[:-4], refs[-4:]
    parts = len(four)
    lines = triple_ref.shape[0]
    local = heads * HD
    width = parts * local
    for piece, k in zip(four, FOUR):
        all_ref[lax.bitwise_xor(place_ref[0], k)] = piece[...].astype(f32)
    for kind in range(3):
        part = jnp.concatenate(
            [
                all_ref[j][: lines + 8, (3 * h + kind) * HD : (3 * h + kind + 1) * HD]
                for j in range(parts)
                for h in range(heads)
            ],
            axis=1,
        )
        triple_ref[:, kind * width : (kind + 1) * width] = part[:lines]
        if kind != 1:
            sums = pltpu.roll(part[lines:], width - turn_ref[0] * lines, 1)
            (queries_ref, None, values_ref)[kind][...] = sums[0, :lines]


def unpack_triple(place, turn, four, heads):
    parts = len(four)
    count, columns = four[0].shape
    lines = count - 16
    S = jax.ShapeDtypeStruct
    V = pl.BlockSpec(memory_space=pltpu.VMEM)
    M = pl.BlockSpec(memory_space=pltpu.SMEM)
    return pl.pallas_call(
        functools.partial(unpack_triple_kernel, heads),
        out_shape=[S((lines, parts * columns), f32), S((lines,), f32), S((lines,), f32)],
        in_specs=[M, M] + [V] * parts,
        out_specs=[V] * 3,
        scratch_shapes=[pltpu.VMEM((parts, count, columns), f32)],
        cost_estimate=SHORT,
        name="unpack_triple",
    )(place, turn, *four)


def gather(v):
    return lax.all_gather(v, "dp", axis=0, tiled=False)


def send(v, shift):
    if shift == 0:
        return v
    parts = lax.axis_size("seq")
    return lax.ppermute(v, "seq", [(i, (i + shift) % parts) for i in range(parts)])


def hop(v, step):
    parts = lax.axis_size("seq")
    return lax.ppermute(v, "seq", [(i, i + step) for i in range(parts) if 0 <= i + step < parts])


def swap(v, bits):
    return lax.ppermute(v, "dp", [(i, i ^ bits) for i in range(lax.axis_size("dp"))])


def double(v, bits):
    return jnp.concatenate([v, swap(v, bits)])


def together(*values):
    return lax.optimization_barrier(values)


def add(a, b):
    return (a.astype(f32) + b.astype(f32)).astype(bf16)


def sum_dp_core(keep, other):
    half = keep.shape[1] // 32 * 16
    a, b = slice(0, half), slice(half, None)
    pick = lambda slots, rows: add(keep[slots, rows], other[slots, rows])
    return (
        pick(slice(0, 2), a),
        pick(slice(2, 4), a),
        pick(slice(0, 4, 2), b),
        pick(slice(1, 4, 2), b),
    )


def sum_dp_first(sums):
    a_keep, a_give, b_keep, b_give = sums
    return (a_keep, swap(a_give, 2), b_keep, swap(b_give, 4))


def sum_dp_second(sums):
    a_keep, a_came, b_keep, b_came = sums
    a, b = add(a_keep, a_came), add(b_keep, b_came)
    return (a[0], a[1], b[0], b[1])


def sum_dp_last(sums):
    a_keep, a_give, b_keep, b_give = sums
    return (a_keep, swap(a_give, 4), b_keep, swap(b_give, 2))


def swap_seq(v, bits):
    return lax.ppermute(v, "seq", [(i, i ^ bits) for i in range(lax.axis_size("seq"))])


def turned_seq(items):
    place = lax.axis_index("seq")
    came = jnp.stack(items)
    return [
        lax.dynamic_index_in_dim(came, lax.bitwise_xor(place, k), keepdims=False)
        for k in range(len(items))
    ]


def sum_seq_first(v):
    v = v.reshape(4, -1, v.shape[1])
    v = turned_seq([v[i] for i in range(4)])
    came = swap_seq(jnp.stack([v[1], v[3]]), 1)
    return add(v[0], came[0]), add(v[2], came[1])


def sum_seq_second(v):
    return add(v[0], swap_seq(v[1], 2))


def rows_of(pieces, dp, width):
    flat = jnp.concatenate(pieces, axis=1)
    pad = -flat.shape[1] % width
    return jnp.pad(flat, ((0, 0), (0, pad))).reshape(dp, -1, width)


def shards(
    layer_input,
    triple_weight,
    query_bias,
    value_bias,
    mixer_weight,
    mixer_bias,
    first_gain,
    first_shift,
    expand_weight,
    expand_bias,
    shrink_weight,
    shrink_bias,
    second_gain,
    second_shift,
    project_weight,
    kept_tokens,
    upstream,
):
    parts = lax.axis_size("seq")
    dp = lax.axis_size("dp")
    place = lax.axis_index("seq")
    mine = lax.axis_index("dp")
    rows = layer_input[0]
    tokens, width = rows.shape
    local = width // parts
    heads = local // HD
    lines = width // dp
    hidden = expand_weight.shape[1]
    hlines = hidden // dp
    emb = project_weight.shape[1]

    fast = dp == 8 and parts == 4 and heads == 3 and lines % 16 == 0
    if not fast:
        blocks = [send(rows, r) for r in range(parts)]

    where = jnp.reshape(place, (1,))
    turn = jnp.reshape(mine, (1,))
    vectors = [
        query_bias,
        value_bias,
        mixer_bias,
        first_gain,
        first_shift,
        shrink_bias,
        second_gain,
        second_shift,
        expand_bias,
    ]
    both = jnp.concatenate([mixer_weight, project_weight], axis=1)
    if fast:
        wide, shrink = jnp.concatenate([expand_weight, both], axis=1)[None], shrink_weight[None]
        own, rest = prepare(where, triple_weight, vectors, parts)
        x_first, y_first = [(0, 2), (4, 6), (1, 3), (5, 7)], [(0, 4), (2, 6), (1, 5), (3, 7)]
        below, above = [rows, hop(rows, 1)], [rows, hop(rows, -1)]
        own = [own] + [swap(own, k) for k in (2, 4, 6)]
        own, above[1], wide = together(own, above[1], wide)
        below[1], shrink = together(below[1], shrink)
        below.append(hop(below[1], 1))
        above.append(hop(above[1], -1))
        own = jnp.stack(own)
        own = [own, swap(own, 1)]
        wide, shrink = double(wide, 2), double(shrink, 4)
        above[2], wide, shrink, own = together(above[2], wide, shrink, own)
        below.append(hop(below[2], 1))
        above.append(hop(above[2], -1))
        w_wide = [wide, swap(wide, 4)]
        w_shrink = [shrink, swap(shrink, 2)]
        w_own, bias, vec, b_expand = assemble(
            where, turn, own, [(0, 2, 4, 6), (1, 3, 5, 7)], parts, dp, hidden
        )
        blocks = [rows] + [
            jnp.where(place >= r, below[r], above[parts - r]) for r in range(1, parts)
        ]
    else:
        turned = jnp.roll(
            triple_weight.reshape(lines, 3, parts, heads, HD), -place, axis=2
        ).transpose(0, 2, 3, 1, 4)
        w_own = gather(turned[:, 0].reshape(lines, 3 * local)).reshape(width, 3 * local)
        w_rest = [gather(turned[:, 1:].swapaxes(1, 2).reshape(lines, -1)).reshape(1, width, -1)]
        small = gather(jnp.concatenate(vectors)).astype(f32)
        vec = jnp.stack([small[:, i * lines : (i + 1) * lines].reshape(width) for i in range(8)])
        b_expand = small[:, 8 * lines :].reshape(1, hidden)
        b_query, b_value = [
            lax.dynamic_slice(vec[i], (place * local,), (local,)).reshape(heads, HD) for i in (0, 1)
        ]
        bias = jnp.stack([b_query, jnp.zeros((heads, HD), f32), b_value], axis=1).reshape(1, -1)
        w_wide = [gather(jnp.concatenate([expand_weight, both], axis=1)).reshape(1, width, -1)]
        w_shrink = [gather(shrink_weight).reshape(1, hidden, width)]
        x_first = y_first = [(0,)]

    joined = [(dot(b, w_own, NN) + bias).astype(bf16) for b in blocks]
    order = list(range(2, parts)) + [1, 0]
    mixed_own = [None] * parts
    stats = [None] * parts
    arrived = [None] * parts
    for i, r in enumerate(order):
        if i > 0:
            joined, mixed_own[order[i - 1]] = together(joined, mixed_own[order[i - 1]])
        if fast and i == 3:
            joined, arrived[order[0]], w_wide[1], w_shrink[1] = together(
                joined, arrived[order[0]], w_wide[1], w_shrink[1]
            )
            late = [swap(w_wide[1], 1), swap(w_shrink[1], 1)]
        if fast and i == 0:
            early = [swap(w_wide[0], 1), swap(w_shrink[0], 1)]
            joined, early = together(joined, early)
        mixed_own[r], stats[r] = attend_forward(joined, r, heads)
        arrived[r] = send(mixed_own[r], -r)
    if fast:
        late, mixed_own[0], arrived = together(late, mixed_own[0], arrived)
        w_wide += [early[0], late[0]]
        w_shrink += [early[1], late[1]]
        rest, arrived, w_wide[3], w_shrink[3] = together(rest[None], arrived, w_wide[3], w_shrink[3])
        rest = double(rest, 2)
    results = feed_forward(
        where,
        turn,
        rows,
        arrived,
        vec,
        b_expand,
        kept_tokens[0].astype(f32)[:, None],
        upstream[0],
        w_wide,
        x_first,
        w_shrink,
        y_first,
    )
    embedded, grad_resid_one, first, active, second, plow, two, lifted, one, sums = results[:10]
    grads = [send(g, r) for r, g in enumerate(results[10:])]

    slabs = hidden // width
    backs = []
    landed = []
    inputs = (joined, grads, mixed_own, stats)

    def backward(h, inputs):
        back = attend_backward(*inputs, h)
        backs.append(back)
        landed.append([send(back[r], -r) for r in range(parts)])

    if fast:
        first, rest = together(first, rest)
        w_rest = [rest, swap(rest, 4)]
        keep, give = weight_grads(
            turn, where, arrived, first, active, second, plow, two, lifted, one, sums, dp
        )
        grads, give, w_rest = together(grads, give, w_rest)
        other = swap(give, 1)
        w_rest += [swap(w, 1) for w in w_rest]
        inputs, keep = together((joined, grads, mixed_own, stats), keep)
        backward(0, inputs)
        keep, other, backs[0] = together(keep, other, backs[0])
        batch = sum_dp_core(keep, other)
        inputs, batch, w_rest = together(inputs, batch, w_rest)
        batch = sum_dp_first(batch)
        backward(1, inputs)
        inputs, landed[0], backs[1] = together(inputs, landed[0], backs[1])
        backward(2, inputs)
        batch, landed[1], backs = together(batch, landed[1], backs)
        batch = sum_dp_second(batch)
        backs, batch = together(backs, batch)
        batch = sum_dp_last(batch)
        keep, give = triple_grads(turn, blocks, backs, dp)
        give, batch, landed[2] = together(give, batch, landed[2])
        halves = [add(batch[0], batch[1]), add(batch[2], batch[3])]
        halves = [sum_seq_first(v) for v in halves]
        last = add(keep, swap(give, 1))
        last = add(last[:2], swap(last[2:], 2))
        last = add(last[0], swap(last[1], 4))
        halves = [sum_seq_second(v) for v in halves]
        halves[1], last = together(halves[1], last)
        last = [last, swap_seq(last, 2)]
        pairs = [jnp.stack([v, swap_seq(v, 2)]) for v in halves]
        pairs[1], last = together(pairs[1], last)
        last += [swap_seq(v, 1) for v in last]
        r_triple, r_queries, r_values = unpack_triple(where, turn, last, heads)
        pairs = [v for pair in pairs for v in (pair, swap_seq(pair, 1))]
        input_grad = input_gradient(turn, grad_resid_one, w_own, landed, w_rest, x_first)
        pairs, r_triple, input_grad = together(pairs, r_triple, input_grad)
        outs = unpack(where, turn, pairs, dp, hidden, emb)
        r_shrink, r_expand, r_mixer, r_project = outs[:4]
        r_offset, r_gamma, r_beta, r_settle, r_gain, r_shift, r_lift = outs[4:]
    else:
        g_expand = dot(first, lifted, TN).astype(bf16)
        mixed = jnp.concatenate(arrived, axis=1)
        g_mixer = jnp.roll(dot(mixed, one, TN).reshape(parts, local, width), place, axis=0)
        g_project = dot(second, plow, TN).astype(bf16)
        batch = jnp.concatenate(
            [
                dot(active, two, TN).astype(bf16).reshape(dp, hlines, width),
                *[
                    g_expand[:, c * width : (c + 1) * width].reshape(dp, lines, width)
                    for c in range(slabs)
                ],
                g_mixer.astype(bf16).reshape(dp, lines, width),
                jnp.stack([rows_of([g[None].reshape(1, -1)], 1, width)[0] for g in g_project.reshape(dp, lines, emb)]),
                jnp.broadcast_to(sums.astype(bf16), (dp,) + sums.shape),
            ],
            axis=1,
        )
        batch = lax.psum_scatter(batch, "dp", scatter_dimension=0, tiled=False)
        batch = lax.psum(batch, "seq")
        for h in range(heads):
            backward(h, inputs)
        g_own = jnp.concatenate([jnp.concatenate(back, axis=0) for back in backs], axis=1)
        g_triple = dot(jnp.concatenate(blocks, axis=0), g_own, TN)
        columns = jnp.sum(g_own.astype(f32), axis=0).astype(bf16)
        last = jnp.concatenate(
            [
                g_triple.astype(bf16).reshape(dp, lines, 3 * local),
                jnp.broadcast_to(columns, (dp, 1, 3 * local)),
            ],
            axis=1,
        )
        last = lax.psum_scatter(last, "dp", scatter_dimension=0, tiled=False)
        last = lax.all_gather(last, "seq", axis=0, tiled=False)
        batch = batch.astype(f32)
        r_shrink = batch[:hlines]
        at = hlines
        r_expand = jnp.concatenate(
            [batch[at + c * lines : at + (c + 1) * lines] for c in range(slabs)], axis=1
        )
        at += lines * slabs
        r_mixer = batch[at : at + lines]
        at += lines
        piece = lines * emb // width
        r_project = batch[at : at + piece].reshape(lines, emb)
        tail = batch[at + piece :]
        r_offset, r_gamma, r_beta, r_settle, r_gain, r_shift = [
            lax.dynamic_slice(tail[i], (mine * lines,), (lines,)) for i in range(6)
        ]
        r_lift = lax.dynamic_slice(
            tail[6 : 6 + slabs].reshape(hidden), (mine * hlines,), (hlines,)
        )

        last = last.astype(f32)
        last = last.reshape(parts, lines + 1, heads, 3, HD).transpose(1, 3, 0, 2, 4)
        r_triple = last[:lines].reshape(lines, 3 * width)
        sums = last[lines].reshape(3, width)
        r_queries = lax.dynamic_slice(sums[0], (mine * lines,), (lines,))
        r_values = lax.dynamic_slice(sums[2], (mine * lines,), (lines,))
        input_grad = input_gradient(turn, grad_resid_one, w_own, landed, w_rest, x_first)
    return (
        embedded[None],
        input_grad[None],
        r_triple,
        r_queries,
        r_values,
        r_mixer,
        r_offset,
        r_gamma,
        r_beta,
        r_expand,
        r_lift,
        r_shrink,
        r_settle,
        r_gain,
        r_shift,
        r_project,
    )


def solution(mesh):
    whole = P("dp", "seq", None)
    rows = P("dp", None)
    flat = P("dp")
    in_specs = (
        whole,
        rows,
        flat,
        flat,
        rows,
        flat,
        flat,
        flat,
        rows,
        flat,
        rows,
        flat,
        flat,
        flat,
        rows,
        P("dp", "seq"),
        whole,
    )
    out_specs = (
        whole,
        whole,
        rows,
        flat,
        flat,
        rows,
        flat,
        flat,
        flat,
        rows,
        flat,
        rows,
        flat,
        flat,
        flat,
        rows,
    )
    return jax.shard_map(shards, mesh=mesh, in_specs=in_specs, out_specs=out_specs, check_vma=False)
```

```python
import functools

import jax
import jax.numpy as jnp
from jax import lax
from jax.experimental import pallas as pl
from jax.experimental.pallas import tpu as pltpu
from jax.sharding import PartitionSpec as P

HD = 64
LOG2E = 1.4426950408889634
f32 = jnp.float32
bf16 = jnp.bfloat16
SHORT = pl.CostEstimate(flops=0, transcendentals=0, bytes_accessed=0)
NT = (((1,), (1,)), ((), ()))
NN = (((1,), (0,)), ((), ()))
TN = (((0,), (0,)), ((), ()))


def dot(a, b, dims):
    return lax.dot_general(a, b, dims, preferred_element_type=f32)


def attend_forward_kernel(parts, block, heads, *refs):
    joined = refs[:parts]
    mixed_ref, stats_ref = refs[parts:]
    count = joined[0].shape[0]
    for h in range(heads):
        base = 3 * HD * h
        query = joined[block][:, base : base + HD] * jnp.asarray(HD**-0.5, bf16)
        scores = [
            dot(query, j[:, base + HD : base + 2 * HD], NT) * LOG2E for j in joined
        ]
        top = jnp.max(scores[0], axis=1, keepdims=True)
        for s in scores[1:]:
            top = jnp.maximum(top, jnp.max(s, axis=1, keepdims=True))
        total = None
        for s, j in zip(scores, joined):
            probs = jnp.exp2(s - top).astype(bf16)
            wide = jnp.concatenate(
                [j[:, base + 2 * HD : base + 3 * HD], jnp.ones((count, HD), bf16)], axis=1
            )
            part = dot(probs, wide, NN)
            total = part if total is None else total + part
        mass = total[:, HD : HD + 1]
        mixed_ref[:, HD * h : HD * (h + 1)] = (total[:, :HD] / mass).astype(bf16)
        stats_ref[:, h : h + 1] = top + jnp.log2(mass)


def attend_forward(joined, block, heads):
    parts = len(joined)
    count = joined[0].shape[0]
    return pl.pallas_call(
        functools.partial(attend_forward_kernel, parts, block, heads),
        out_shape=[
            jax.ShapeDtypeStruct((count, heads * HD), bf16),
            jax.ShapeDtypeStruct((count, 8), f32),
        ],
        in_specs=[pl.BlockSpec(memory_space=pltpu.VMEM)] * parts,
        out_specs=[pl.BlockSpec(memory_space=pltpu.VMEM)] * 2,
        compiler_params=pltpu.CompilerParams(vmem_limit_bytes=40 << 20),
        cost_estimate=SHORT,
        name="attend_forward",
    )(*joined)


def attend_backward_kernel(parts, h, *refs):
    joined = refs[:parts]
    grads = refs[parts : 2 * parts]
    mixed = refs[2 * parts : 3 * parts]
    stats = refs[3 * parts : 4 * parts]
    outs = refs[4 * parts : 5 * parts]
    keys_sum, values_sum = refs[5 * parts :]
    base = 3 * HD * h
    count = joined[0].shape[0]
    for b in range(parts):
        query = joined[b][:, base : base + HD] * jnp.asarray(HD**-0.5, bf16)
        grad = grads[b][:, HD * h : HD * (h + 1)]
        inner = jnp.sum(
            grad.astype(f32) * mixed[b][:, HD * h : HD * (h + 1)].astype(f32), axis=1, keepdims=True
        )
        level = stats[b][:, h : h + 1]
        query_t = query.T
        grad_t = grad.T
        total = None
        for c in range(parts):
            keys = joined[c][:, base + HD : base + 2 * HD]
            values = joined[c][:, base + 2 * HD : base + 3 * HD]
            probs = jnp.exp2(dot(query, keys, NT) * LOG2E - level)
            grad_probs = dot(grad, values, NT)
            grad_scores = (probs * (grad_probs - inner)).astype(bf16)
            part = dot(grad_scores, keys, NN)
            total = part if total is None else total + part
            span = slice(c * count, (c + 1) * count)
            grad_values = dot(grad_t, probs.astype(bf16), NN)
            grad_keys = dot(query_t, grad_scores, NN)
            if b == 0:
                values_sum[:, span] = grad_values
                keys_sum[:, span] = grad_keys
            else:
                values_sum[:, span] += grad_values
                keys_sum[:, span] += grad_keys
        outs[b][:, :HD] = (total * HD**-0.5).astype(bf16)
    for c in range(parts):
        span = slice(c * count, (c + 1) * count)
        outs[c][:, HD : 2 * HD] = keys_sum[:, span].T.astype(bf16)
        outs[c][:, 2 * HD :] = values_sum[:, span].T.astype(bf16)


def attend_backward(joined, grads, mixed, stats, h):
    parts = len(joined)
    count = joined[0].shape[0]
    return pl.pallas_call(
        functools.partial(attend_backward_kernel, parts, h),
        out_shape=[jax.ShapeDtypeStruct((count, 3 * HD), bf16)] * parts,
        grid=(1,),
        scratch_shapes=[pltpu.VMEM((HD, parts * count), f32)] * 2,
        compiler_params=pltpu.CompilerParams(vmem_limit_bytes=60 << 20),
        cost_estimate=SHORT,
        name="attend_backward",
    )(*joined, *grads, *mixed, *stats)


def normal_cdf_and_density(x):
    a = jnp.abs(x) * (0.5**0.5)
    t = 1.0 / (1.0 + 0.5 * a)
    series = -0.82215223 + t * 0.17087277
    for c in (1.48851587, -1.13520398, 0.27886807, -0.18628806, 0.09678418, 0.37409196, 1.00002368):
        series = c + t * series
    tail = 0.5 * t * jnp.exp(-a * a - 1.26551223 + t * series)
    cdf = jnp.where(x >= 0, 1.0 - tail, tail)
    return cdf, jnp.exp(-0.5 * x * x) * 0.3989422804014327


def standardize(rows):
    mean = jnp.mean(rows, axis=-1, keepdims=True)
    centred = rows - mean
    spread = jnp.mean(centred * centred, axis=-1, keepdims=True)
    scale = lax.rsqrt(spread + 1e-12)
    return centred * scale, scale


def norm_back(grad, gain, normed, scale):
    g = grad * gain
    return (
        g
        - jnp.mean(g, axis=-1, keepdims=True)
        - normed * jnp.mean(g * normed, axis=-1, keepdims=True)
    ) * scale


def ffn_kernel(parts, step, wide_from, shrink_from, place_ref, turn_ref, *refs):
    rows_ref, arrived, refs = refs[0], refs[1 : 1 + parts], refs[1 + parts :]
    vec_ref, lift_bias_ref, keep_ref, ct_ref = refs[:4]
    groups = len(wide_from)
    wide_hbm, shrink_hbm = refs[4 : 4 + groups], refs[4 + groups : 4 + 2 * groups]
    outs = refs[4 + 2 * groups :]
    (embedded_ref, resid_ref, first_ref, active_ref, second_ref, plow_ref, two_ref, lifted_ref, one_ref, sums_ref) = outs[:10]
    mixed_grads = outs[10 : 10 + parts]
    mixer_ref, expand_ref, shrink_ref, slope_ref, total_ref, sems = outs[10 + parts :]
    width = rows_ref.shape[1]
    hidden = lift_bias_ref.shape[1]
    local = width // parts
    chunks = hidden // step
    place = place_ref[0]

    pieces = sum(len(f) for f in wide_from)

    def load(sources, origin, columns, target, first):
        count = target.shape[0] // pieces
        copies = []
        for source, ks in zip(sources, origin):
            for i, k in enumerate(ks):
                at = pl.multiple_of(lax.bitwise_xor(turn_ref[0], k) * count, count) if pieces > 1 else 0
                copies.append(
                    pltpu.make_async_copy(
                        source.at[i, :, columns],
                        target.at[pl.ds(at, count), :],
                        sems.at[first + len(copies)],
                    )
                )
                copies[-1].start()
        return copies

    side = width + ct_ref.shape[1]
    load_mixer = load(wide_hbm, wide_from, slice(hidden, hidden + side), mixer_ref, 0)
    load_expand = load(wide_hbm, wide_from, slice(0, hidden), expand_ref, pieces)
    load_shrink = load(shrink_hbm, shrink_from, slice(0, width), shrink_ref, 2 * pieces)

    def vec(i):
        return vec_ref[i : i + 1, :]

    def mixer_rows(r):
        at = lax.rem(place + r, parts) * local
        return mixer_ref[pl.ds(pl.multiple_of(at, local), local), :width]

    for copy in load_mixer:
        copy.wait()
    branch = vec(2)
    for r in range(parts):
        branch = branch + dot(arrived[r][...], mixer_rows(r), NN)
    normed_one, scale_one = standardize(rows_ref[...].astype(f32) + branch)
    first = normed_one * vec(3) + vec(4)
    first_low = first.astype(bf16)
    first_ref[...] = first_low
    total_ref[...] = first + vec(5)

    for copy in load_expand + load_shrink:
        copy.wait()

    def forward(c, carry):
        at = pl.multiple_of(c * step, step)
        lifted = dot(first_ref[...], expand_ref[:, pl.ds(at, step)], NN) + lift_bias_ref[:, pl.ds(at, step)]
        cdf, density = normal_cdf_and_density(lifted)
        active = (lifted * cdf).astype(bf16)
        active_ref[:, pl.ds(at, step)] = active
        slope_ref[:, pl.ds(at, step)] = cdf + lifted * density
        total_ref[...] += dot(active, shrink_ref[pl.ds(at, step), :], NN)
        return carry

    lax.fori_loop(0, chunks, forward, 0, unroll=True)

    normed_two, scale_two = standardize(total_ref[...])
    second_low = (normed_two * vec(6) + vec(7)).astype(bf16)
    second_ref[...] = second_low
    w_project = mixer_ref[:, width:]
    projected = dot(second_low, w_project, NN)
    keep = keep_ref[...]
    inverse = lax.rsqrt(jnp.sum(projected * projected, axis=-1, keepdims=True) + 1e-06)
    unit = projected * inverse
    embedded_ref[...] = unit * keep
    ct = ct_ref[...]
    plow = (keep * (ct - unit * jnp.sum(unit * ct, axis=-1, keepdims=True)) * inverse).astype(bf16)
    plow_ref[...] = plow
    grad_second = dot(plow, w_project, NT)
    sums_ref[4:5, :] = jnp.sum(grad_second * normed_two, axis=0, keepdims=True)
    sums_ref[5:6, :] = jnp.sum(grad_second, axis=0, keepdims=True)
    grad_two = norm_back(grad_second, vec(6), normed_two, scale_two)
    two_low = grad_two.astype(bf16)
    two_ref[...] = two_low
    sums_ref[3:4, :] = jnp.sum(two_low.astype(f32), axis=0, keepdims=True)
    total_ref[...] = grad_two

    def backward(c, carry):
        at = pl.multiple_of(c * step, step)
        grad_active = dot(two_ref[...], shrink_ref[pl.ds(at, step), :], NT)
        low = (grad_active * slope_ref[:, pl.ds(at, step)]).astype(bf16)
        lifted_ref[:, pl.ds(at, step)] = low
        total_ref[...] += dot(low, expand_ref[:, pl.ds(at, step)], NT)
        return carry

    lax.fori_loop(0, chunks, backward, 0, unroll=True)
    for c in range(hidden // width):
        sums_ref[6 + c : 7 + c, :] = jnp.sum(
            lifted_ref[:, c * width : (c + 1) * width].astype(f32), axis=0, keepdims=True
        )

    grad_first = total_ref[...]
    sums_ref[1:2, :] = jnp.sum(grad_first * normed_one, axis=0, keepdims=True)
    sums_ref[2:3, :] = jnp.sum(grad_first, axis=0, keepdims=True)
    grad_one = norm_back(grad_first, vec(3), normed_one, scale_one)
    resid_ref[...] = grad_one
    one_low = grad_one.astype(bf16)
    one_ref[...] = one_low
    sums_ref[0:1, :] = jnp.sum(one_low.astype(f32), axis=0, keepdims=True)
    for r in range(parts):
        mixed_grads[r][...] = dot(one_low, mixer_rows(r), NT).astype(bf16)
    used = 6 + hidden // width
    sums_ref[used:, :] = jnp.zeros((sums_ref.shape[0] - used, width), f32)


def feed_forward(place, turn, rows, arrived, vec, lift_bias, keep, ct, wide, wide_from, shrink, shrink_from):
    parts = len(arrived)
    groups = len(wide)
    pieces = sum(len(f) for f in wide_from)
    tokens, width = rows.shape
    hidden = lift_bias.shape[1]
    emb = ct.shape[1]
    local = width // parts
    V = pl.BlockSpec(memory_space=pltpu.VMEM)
    A = pl.BlockSpec(memory_space=pl.ANY)
    M = pl.BlockSpec(memory_space=pltpu.SMEM)
    S = jax.ShapeDtypeStruct
    return pl.pallas_call(
        functools.partial(ffn_kernel, parts, hidden // 4, wide_from, shrink_from),
        out_shape=[
            S((tokens, emb), f32),
            S((tokens, width), f32),
            S((tokens, width), bf16),
            S((tokens, hidden), bf16),
            S((tokens, width), bf16),
            S((tokens, emb), bf16),
            S((tokens, width), bf16),
            S((tokens, hidden), bf16),
            S((tokens, width), bf16),
            S((16, width), f32),
        ]
        + [S((tokens, local), bf16)] * parts,
        in_specs=[M, M, V] + [V] * parts + [V] * 4 + [A] * (2 * groups),
        out_specs=[V] * (10 + parts),
        scratch_shapes=[
            pltpu.VMEM((width, width + emb), bf16),
            pltpu.VMEM((width, hidden), bf16),
            pltpu.VMEM((hidden, width), bf16),
            pltpu.VMEM((tokens, hidden), f32),
            pltpu.VMEM((tokens, width), f32),
            pltpu.SemaphoreType.DMA((3 * pieces,)),
        ],
        compiler_params=pltpu.CompilerParams(vmem_limit_bytes=56 << 20),
        cost_estimate=SHORT,
        name="feed_forward",
    )(place, turn, rows, *arrived, vec, lift_bias, keep, ct, *wide, *shrink)


def prepare_kernel(parts, heads, place_ref, triple_ref, *refs):
    vectors, (own_ref, rest_ref) = refs[:-2], refs[-2:]
    lines = triple_ref.shape[0]
    local = heads * HD
    width = parts * local
    shift = lax.rem(parts - place_ref[0], parts) * local
    kinds = [
        pltpu.roll(triple_ref[:, i * width : (i + 1) * width].astype(f32), shift, 1).astype(bf16)
        for i in range(3)
    ]
    for h in range(heads):
        for r in range(parts):
            piece = jnp.concatenate(
                [k[:, r * local + h * HD : r * local + (h + 1) * HD] for k in kinds], axis=1
            )
            if r == 0:
                own_ref[:lines, h * 3 * HD : (h + 1) * 3 * HD] = piece
            else:
                at = (h * (parts - 1) + r - 1) * 3 * HD
                rest_ref[:, at : at + 3 * HD] = piece
    lane = own_ref.shape[1]
    lined = [jnp.zeros((16 - len(vectors), lane), f32)]
    for v in vectors[::-1]:
        line = v[...].astype(f32).reshape(1, -1)
        lined.insert(0, jnp.pad(line, ((0, 0), (0, lane - line.shape[1]))))
    own_ref[lines:, :] = jnp.concatenate(lined).astype(bf16)


def prepare(place, triple, vectors, parts):
    lines, columns = triple.shape
    own = columns // parts
    V = pl.BlockSpec(memory_space=pltpu.VMEM)
    return pl.pallas_call(
        functools.partial(prepare_kernel, parts, own // (3 * HD)),
        out_shape=[
            jax.ShapeDtypeStruct((lines + 16, own), bf16),
            jax.ShapeDtypeStruct((lines, columns - own), bf16),
        ],
        in_specs=[pl.BlockSpec(memory_space=pltpu.SMEM), V] + [V] * len(vectors),
        out_specs=[V] * 2,
        cost_estimate=SHORT,
        name="prepare",
    )(place, triple, *vectors)


def assemble_kernel(parts, origin, place_ref, turn_ref, *refs):
    stacks, (w_ref, bias_ref, vec_ref, lift_ref, all_ref) = refs[:-5], refs[-5:]
    dp = all_ref.shape[0]
    lines = w_ref.shape[0] // dp
    hlines = lift_ref.shape[1] // dp
    width = vec_ref.shape[1]
    local = width // parts
    for stack, ks in zip(stacks, origin):
        for i, k in enumerate(ks):
            s = lax.bitwise_xor(turn_ref[0], k)
            w_ref[pl.ds(pl.multiple_of(s * lines, lines), lines), :] = stack[i, :lines, :]
            all_ref[s] = stack[i, lines:, :].astype(f32)
    vec_ref[...] = jnp.concatenate([all_ref[s][:8, :lines] for s in range(dp)], axis=1)
    lift_ref[...] = jnp.concatenate([all_ref[s][8:9, :hlines] for s in range(dp)], axis=1)
    shift = lax.rem(parts - place_ref[0], parts) * local
    turned = pltpu.roll(vec_ref[...], shift, 1)
    pieces = []
    for at in range(0, local, HD):
        pieces += [turned[0:1, at : at + HD], jnp.zeros((1, HD), f32), turned[1:2, at : at + HD]]
    bias_ref[...] = jnp.concatenate(pieces, axis=1)


def assemble(place, turn, stacks, origin, parts, dp, hidden):
    count, own = stacks[0].shape[1:]
    width = (count - 16) * dp
    V = pl.BlockSpec(memory_space=pltpu.VMEM)
    M = pl.BlockSpec(memory_space=pltpu.SMEM)
    return pl.pallas_call(
        functools.partial(assemble_kernel, parts, origin),
        out_shape=[
            jax.ShapeDtypeStruct((width, own), bf16),
            jax.ShapeDtypeStruct((1, own), f32),
            jax.ShapeDtypeStruct((8, width), f32),
            jax.ShapeDtypeStruct((1, hidden), f32),
        ],
        in_specs=[M, M] + [V] * len(stacks),
        out_specs=[V] * 4,
        scratch_shapes=[pltpu.VMEM((dp, 16, own), f32)],
        cost_estimate=SHORT,
        name="assemble",
    )(place, turn, *stacks)


def input_grad_kernel(origin, parts, heads, turn_ref, resid_ref, own_ref, *refs):
    landed, refs = refs[: heads * parts], refs[heads * parts :]
    stacks, (out_ref, rest_ref) = refs[: len(origin)], refs[len(origin) :]
    pieces = sum(len(ks) for ks in origin)
    count = rest_ref.shape[0] // pieces
    for source, ks in zip(stacks, origin):
        for i, k in enumerate(ks):
            at = pl.multiple_of(lax.bitwise_xor(turn_ref[0], k) * count, count) if pieces > 1 else 0
            rest_ref[pl.ds(at, count), :] = source[i]
    near = jnp.concatenate([landed[h * parts][...] for h in range(heads)], axis=1)
    far = jnp.concatenate(
        [landed[h * parts + r][...] for h in range(heads) for r in range(1, parts)], axis=1
    )
    out_ref[...] = resid_ref[...] + dot(near, own_ref[...], NT) + dot(far, rest_ref[...], NT)


def input_gradient(turn, resid, w_own, landed, stacks, origin):
    heads, parts = len(landed), len(landed[0])
    W = pl.BlockSpec()
    return pl.pallas_call(
        functools.partial(input_grad_kernel, origin, parts, heads),
        grid=(1,),
        out_shape=jax.ShapeDtypeStruct(resid.shape, f32),
        in_specs=[pl.BlockSpec(memory_space=pltpu.SMEM)] + [W] * (2 + heads * parts + len(stacks)),
        out_specs=W,
        scratch_shapes=[pltpu.VMEM((resid.shape[1], stacks[0].shape[2]), bf16)],
        compiler_params=pltpu.CompilerParams(vmem_limit_bytes=60 << 20),
        cost_estimate=SHORT,
        name="input_gradient",
    )(turn, resid, w_own, *[v for h in landed for v in h], *stacks)


def put(keep_ref, give_ref, k, rows, columns, value):
    place = 2 * lax.bitwise_and(lax.shift_right_logical(k, 1), 1) + lax.shift_right_logical(k, 2)

    @pl.when(lax.bitwise_and(k, 1) == 0)
    def _():
        keep_ref[place, rows, columns] = value

    @pl.when(lax.bitwise_and(k, 1) == 1)
    def _():
        give_ref[place, rows, columns] = value


def weight_grads_kernel(parts, dp, turn_ref, place_ref, *refs):
    arrived = refs[:parts]
    first_ref, active_ref, second_ref, plow_ref, two_ref, lifted_ref, one_ref, sums_ref = refs[parts : parts + 8]
    keep_ref, give_ref, out_ref, sems = refs[parts + 8 :]
    width = first_ref.shape[1]
    hidden = active_ref.shape[1]
    emb = plow_ref.shape[1]
    lines, hlines, local = width // dp, hidden // dp, width // parts
    turn = turn_ref[0]
    place = place_ref[0]
    slabs = hidden // width
    base_mixer = hlines + lines * slabs
    base_project = base_mixer + lines
    piece = lines * emb // width
    base_vec = base_project + piece

    def leave(stage, at, count):
        for s in range(dp):
            k = lax.bitwise_xor(turn, s)
            slot = 2 * lax.bitwise_and(lax.shift_right_logical(k, 1), 1) + lax.shift_right_logical(k, 2)
            source = out_ref.at[s, pl.ds(at, count)]
            sem = sems.at[stage, s]

            @pl.when(lax.bitwise_and(k, 1) == 0)
            def _():
                pltpu.make_async_copy(source, keep_ref.at[slot, pl.ds(at, count)], sem).start()

            @pl.when(lax.bitwise_and(k, 1) == 1)
            def _():
                pltpu.make_async_copy(source, give_ref.at[slot, pl.ds(at, count)], sem).start()

    two = two_ref[...]
    per = width // hlines
    for c in range(slabs):
        part = dot(active_ref[:, c * width : (c + 1) * width], two, TN).astype(bf16)
        for i in range(per):
            out_ref[c * per + i, :hlines, :] = part[i * hlines : (i + 1) * hlines]
    leave(0, 0, hlines)
    first = first_ref[...]
    for c in range(slabs):
        part = dot(first, lifted_ref[:, c * width : (c + 1) * width], TN).astype(bf16)
        at = hlines + c * lines
        for s in range(dp):
            out_ref[s, at : at + lines, :] = part[s * lines : (s + 1) * lines]
    leave(1, hlines, base_mixer - hlines)
    vectors = sums_ref[...].astype(bf16)
    part = dot(second_ref[...], plow_ref[...], TN).astype(bf16)
    for s in range(dp):
        for a in range(width // emb):
            at = s * lines + a * piece
            out_ref[s, base_project : base_project + piece, a * emb : (a + 1) * emb] = part[at : at + piece]
        out_ref[s, base_vec : base_vec + 16, :] = vectors
    one = one_ref[...]
    per = local // lines
    for r in range(parts):
        part = dot(arrived[r][...], one, TN).astype(bf16)
        j = lax.rem(place + r, parts)
        for i in range(per):
            out_ref[j * per + i, base_mixer : base_mixer + lines, :] = part[i * lines : (i + 1) * lines]
    rest = base_vec + 16 - base_mixer
    leave(2, base_mixer, rest)
    for stage, (at, count) in enumerate(
        ((0, hlines), (hlines, base_mixer - hlines), (base_mixer, rest))
    ):
        for s in range(dp):
            pltpu.make_async_copy(
                out_ref.at[s, pl.ds(at, count)], keep_ref.at[0, pl.ds(at, count)], sems.at[stage, s]
            ).wait()


def weight_grads(turn, place, arrived, first, active, second, plow, two, lifted, one, sums, dp):
    parts = len(arrived)
    tokens, width = first.shape
    hidden = active.shape[1]
    emb = plow.shape[1]
    lines, hlines = width // dp, hidden // dp
    total = hlines + lines * (hidden // width) + lines + lines * emb // width + 16
    V = pl.BlockSpec(memory_space=pltpu.VMEM)
    M = pl.BlockSpec(memory_space=pltpu.SMEM)
    return pl.pallas_call(
        functools.partial(weight_grads_kernel, parts, dp),
        out_shape=[jax.ShapeDtypeStruct((dp // 2, total, width), bf16)] * 2,
        in_specs=[M, M] + [V] * (parts + 8),
        out_specs=[pl.BlockSpec(memory_space=pl.ANY)] * 2,
        scratch_shapes=[pltpu.VMEM((dp, total, width), bf16), pltpu.SemaphoreType.DMA((3, dp))],
        compiler_params=pltpu.CompilerParams(vmem_limit_bytes=56 << 20),
        cost_estimate=SHORT,
        name="weight_grads",
    )(turn, place, *arrived, first, active, second, plow, two, lifted, one, sums)


def triple_grads_kernel(parts, heads, dp, turn_ref, *refs):
    blocks = refs[:parts]
    backs = refs[parts : parts + heads * parts]
    keep_ref, give_ref = refs[parts + heads * parts :]
    width = blocks[0].shape[1]
    lines = width // dp
    turn = turn_ref[0]
    ones = jnp.ones((16, blocks[0].shape[0]), bf16)
    total = sums = None
    for r in range(parts):
        grad = jnp.concatenate([backs[h * parts + r][...] for h in range(heads)], axis=1)
        part, line = dot(blocks[r][...], grad, TN), dot(ones, grad, NN)
        total = part if r == 0 else total + part
        sums = line if r == 0 else sums + line
    total, sums = total.astype(bf16), sums.astype(bf16)
    columns = slice(0, total.shape[1])
    for s in range(dp):
        k = lax.bitwise_xor(turn, s)
        put(keep_ref, give_ref, k, slice(0, lines), columns, total[s * lines : (s + 1) * lines])
        put(keep_ref, give_ref, k, slice(lines, lines + 16), columns, sums)


def triple_grads(turn, blocks, backs, dp):
    parts, heads = len(blocks), len(backs)
    count, width = blocks[0].shape
    V = pl.BlockSpec(memory_space=pltpu.VMEM)
    return pl.pallas_call(
        functools.partial(triple_grads_kernel, parts, heads, dp),
        out_shape=[jax.ShapeDtypeStruct((dp // 2, width // dp + 16, 3 * HD * heads), bf16)] * 2,
        in_specs=[pl.BlockSpec(memory_space=pltpu.SMEM)] + [V] * (parts + heads * parts),
        out_specs=[V] * 2,
        compiler_params=pltpu.CompilerParams(vmem_limit_bytes=56 << 20),
        cost_estimate=SHORT,
        name="triple_grads",
    )(turn, *blocks, *[b for back in backs for b in back])


FOUR = (0, 2, 1, 3)


def unpack_kernel(slabs, place_ref, turn_ref, *refs):
    pairs, outs, all_ref = refs[:4], refs[4:-1], refs[-1]
    shrink_ref, expand_ref, mixer_ref, project_ref = outs[:4]
    count, width = pairs[0].shape[1:]
    for half in range(2):
        for i, k in enumerate(FOUR):
            at = (4 * half + lax.bitwise_xor(place_ref[0], k)) * count
            piece = pairs[2 * half + i // 2][i % 2]
            all_ref[pl.ds(pl.multiple_of(at, count), count), :] = piece.astype(f32)
    lines, emb = project_ref.shape
    at = shrink_ref.shape[0]
    shrink_ref[...] = all_ref[:at, :]
    for c in range(slabs):
        expand_ref[:, c * width : (c + 1) * width] = all_ref[at : at + lines, :]
        at += lines
    mixer_ref[...] = all_ref[at : at + lines, :]
    at += lines
    piece = lines * emb // width
    for a in range(width // emb):
        project_ref[a * piece : (a + 1) * piece, :] = all_ref[at : at + piece, a * emb : (a + 1) * emb]
    at += piece
    mine = turn_ref[0]
    turned = pltpu.roll(all_ref[at : at + 8, :], width - mine * lines, 1)
    for i in range(6):
        outs[4 + i][...] = turned[i, :lines]
    hlines = outs[10].shape[0]
    per = width // hlines
    line = all_ref[pl.ds(at + 6 + lax.div(mine, per), 1), :]
    line = jnp.broadcast_to(line, (8, width))
    outs[10][...] = pltpu.roll(line, width - lax.rem(mine, per) * hlines, 1)[0, :hlines]


def unpack(place, turn, pairs, dp, hidden, emb):
    count, width = pairs[0].shape[1:]
    lines, hlines = width // dp, hidden // dp
    S = jax.ShapeDtypeStruct
    V = pl.BlockSpec(memory_space=pltpu.VMEM)
    M = pl.BlockSpec(memory_space=pltpu.SMEM)
    return pl.pallas_call(
        functools.partial(unpack_kernel, hidden // width),
        out_shape=[
            S((hlines, width), f32),
            S((lines, hidden), f32),
            S((lines, width), f32),
            S((lines, emb), f32),
        ]
        + [S((lines,), f32)] * 6
        + [S((hlines,), f32)],
        in_specs=[M, M] + [V] * 4,
        out_specs=[V] * 11,
        scratch_shapes=[pltpu.VMEM((8 * count, width), f32)],
        cost_estimate=SHORT,
        name="unpack",
    )(place, turn, *pairs)


def unpack_triple_kernel(heads, place_ref, turn_ref, *refs):
    four, (triple_ref, queries_ref, values_ref, all_ref) = refs[:-4], refs[-4:]
    parts = len(four)
    lines = triple_ref.shape[0]
    local = heads * HD
    width = parts * local
    for piece, k in zip(four, FOUR):
        all_ref[lax.bitwise_xor(place_ref[0], k)] = piece[...].astype(f32)
    for kind in range(3):
        part = jnp.concatenate(
            [
                all_ref[j][: lines + 8, (3 * h + kind) * HD : (3 * h + kind + 1) * HD]
                for j in range(parts)
                for h in range(heads)
            ],
            axis=1,
        )
        triple_ref[:, kind * width : (kind + 1) * width] = part[:lines]
        if kind != 1:
            sums = pltpu.roll(part[lines:], width - turn_ref[0] * lines, 1)
            (queries_ref, None, values_ref)[kind][...] = sums[0, :lines]


def unpack_triple(place, turn, four, heads):
    parts = len(four)
    count, columns = four[0].shape
    lines = count - 16
    S = jax.ShapeDtypeStruct
    V = pl.BlockSpec(memory_space=pltpu.VMEM)
    M = pl.BlockSpec(memory_space=pltpu.SMEM)
    return pl.pallas_call(
        functools.partial(unpack_triple_kernel, heads),
        out_shape=[S((lines, parts * columns), f32), S((lines,), f32), S((lines,), f32)],
        in_specs=[M, M] + [V] * parts,
        out_specs=[V] * 3,
        scratch_shapes=[pltpu.VMEM((parts, count, columns), f32)],
        cost_estimate=SHORT,
        name="unpack_triple",
    )(place, turn, *four)


def gather(v):
    return lax.all_gather(v, "dp", axis=0, tiled=False)


def send(v, shift):
    if shift == 0:
        return v
    parts = lax.axis_size("seq")
    return lax.ppermute(v, "seq", [(i, (i + shift) % parts) for i in range(parts)])


def hop(v, step):
    parts = lax.axis_size("seq")
    return lax.ppermute(v, "seq", [(i, i + step) for i in range(parts) if 0 <= i + step < parts])


def swap(v, bits):
    return lax.ppermute(v, "dp", [(i, i ^ bits) for i in range(lax.axis_size("dp"))])


def double(v, bits):
    return jnp.concatenate([v, swap(v, bits)])


def together(*values):
    return lax.optimization_barrier(values)


def add(a, b):
    return (a.astype(f32) + b.astype(f32)).astype(bf16)


def sum_dp_core(keep, other):
    half = keep.shape[1] // 32 * 16
    a, b = slice(0, half), slice(half, None)
    pick = lambda slots, rows: add(keep[slots, rows], other[slots, rows])
    return (
        pick(slice(0, 2), a),
        pick(slice(2, 4), a),
        pick(slice(0, 4, 2), b),
        pick(slice(1, 4, 2), b),
    )


def sum_dp_first(sums):
    a_keep, a_give, b_keep, b_give = sums
    return (a_keep, swap(a_give, 2), b_keep, swap(b_give, 4))


def sum_dp_second(sums):
    a_keep, a_came, b_keep, b_came = sums
    a, b = add(a_keep, a_came), add(b_keep, b_came)
    return (a[0], a[1], b[0], b[1])


def sum_dp_last(sums):
    a_keep, a_give, b_keep, b_give = sums
    return (a_keep, swap(a_give, 4), b_keep, swap(b_give, 2))


def swap_seq(v, bits):
    return lax.ppermute(v, "seq", [(i, i ^ bits) for i in range(lax.axis_size("seq"))])


def turned_seq(items):
    place = lax.axis_index("seq")
    came = jnp.stack(items)
    return [
        lax.dynamic_index_in_dim(came, lax.bitwise_xor(place, k), keepdims=False)
        for k in range(len(items))
    ]


def sum_seq_first(v):
    v = v.reshape(4, -1, v.shape[1])
    v = turned_seq([v[i] for i in range(4)])
    came = swap_seq(jnp.stack([v[1], v[3]]), 1)
    return add(v[0], came[0]), add(v[2], came[1])


def sum_seq_second(v):
    return add(v[0], swap_seq(v[1], 2))


def rows_of(pieces, dp, width):
    flat = jnp.concatenate(pieces, axis=1)
    pad = -flat.shape[1] % width
    return jnp.pad(flat, ((0, 0), (0, pad))).reshape(dp, -1, width)


def shards(
    layer_input,
    triple_weight,
    query_bias,
    value_bias,
    mixer_weight,
    mixer_bias,
    first_gain,
    first_shift,
    expand_weight,
    expand_bias,
    shrink_weight,
    shrink_bias,
    second_gain,
    second_shift,
    project_weight,
    kept_tokens,
    upstream,
):
    parts = lax.axis_size("seq")
    dp = lax.axis_size("dp")
    place = lax.axis_index("seq")
    mine = lax.axis_index("dp")
    rows = layer_input[0]
    tokens, width = rows.shape
    local = width // parts
    heads = local // HD
    lines = width // dp
    hidden = expand_weight.shape[1]
    hlines = hidden // dp
    emb = project_weight.shape[1]

    fast = dp == 8 and parts == 4 and heads == 3 and lines % 16 == 0
    if not fast:
        blocks = [send(rows, r) for r in range(parts)]

    where = jnp.reshape(place, (1,))
    turn = jnp.reshape(mine, (1,))
    vectors = [
        query_bias,
        value_bias,
        mixer_bias,
        first_gain,
        first_shift,
        shrink_bias,
        second_gain,
        second_shift,
        expand_bias,
    ]
    both = jnp.concatenate([mixer_weight, project_weight], axis=1)
    if fast:
        wide, shrink = jnp.concatenate([expand_weight, both], axis=1)[None], shrink_weight[None]
        own, rest = prepare(where, triple_weight, vectors, parts)
        x_first, y_first = [(0, 2), (4, 6), (1, 3), (5, 7)], [(0, 4), (2, 6), (1, 5), (3, 7)]
        below, above = [rows, hop(rows, 1)], [rows, hop(rows, -1)]
        own = [own] + [swap(own, k) for k in (2, 4, 6)]
        own, above[1], wide = together(own, above[1], wide)
        below[1], shrink = together(below[1], shrink)
        below.append(hop(below[1], 1))
        above.append(hop(above[1], -1))
        own = jnp.stack(own)
        own = [own, swap(own, 1)]
        wide, shrink = double(wide, 2), double(shrink, 4)
        above[2], wide, shrink, own = together(above[2], wide, shrink, own)
        below.append(hop(below[2], 1))
        above.append(hop(above[2], -1))
        w_wide = [wide, swap(wide, 4)]
        w_shrink = [shrink, swap(shrink, 2)]
        w_own, bias, vec, b_expand = assemble(
            where, turn, own, [(0, 2, 4, 6), (1, 3, 5, 7)], parts, dp, hidden
        )
        blocks = [rows] + [
            jnp.where(place >= r, below[r], above[parts - r]) for r in range(1, parts)
        ]
    else:
        turned = jnp.roll(
            triple_weight.reshape(lines, 3, parts, heads, HD), -place, axis=2
        ).transpose(0, 2, 3, 1, 4)
        w_own = gather(turned[:, 0].reshape(lines, 3 * local)).reshape(width, 3 * local)
        w_rest = [gather(turned[:, 1:].swapaxes(1, 2).reshape(lines, -1)).reshape(1, width, -1)]
        small = gather(jnp.concatenate(vectors)).astype(f32)
        vec = jnp.stack([small[:, i * lines : (i + 1) * lines].reshape(width) for i in range(8)])
        b_expand = small[:, 8 * lines :].reshape(1, hidden)
        b_query, b_value = [
            lax.dynamic_slice(vec[i], (place * local,), (local,)).reshape(heads, HD) for i in (0, 1)
        ]
        bias = jnp.stack([b_query, jnp.zeros((heads, HD), f32), b_value], axis=1).reshape(1, -1)
        w_wide = [gather(jnp.concatenate([expand_weight, both], axis=1)).reshape(1, width, -1)]
        w_shrink = [gather(shrink_weight).reshape(1, hidden, width)]
        x_first = y_first = [(0,)]

    joined = [(dot(b, w_own, NN) + bias).astype(bf16) for b in blocks]
    order = list(range(2, parts)) + [1, 0]
    mixed_own = [None] * parts
    stats = [None] * parts
    arrived = [None] * parts
    for i, r in enumerate(order):
        if i > 0:
            joined, mixed_own[order[i - 1]] = together(joined, mixed_own[order[i - 1]])
        if fast and i == 3:
            joined, arrived[order[0]], w_wide[1], w_shrink[1] = together(
                joined, arrived[order[0]], w_wide[1], w_shrink[1]
            )
            late = [swap(w_wide[1], 1), swap(w_shrink[1], 1)]
        if fast and i == 0:
            early = [swap(w_wide[0], 1), swap(w_shrink[0], 1)]
            joined, early = together(joined, early)
        mixed_own[r], stats[r] = attend_forward(joined, r, heads)
        arrived[r] = send(mixed_own[r], -r)
    if fast:
        late, mixed_own[0], arrived = together(late, mixed_own[0], arrived)
        w_wide += [early[0], late[0]]
        w_shrink += [early[1], late[1]]
        rest, arrived, w_wide[3], w_shrink[3] = together(rest[None], arrived, w_wide[3], w_shrink[3])
        rest = double(rest, 2)
    results = feed_forward(
        where,
        turn,
        rows,
        arrived,
        vec,
        b_expand,
        kept_tokens[0].astype(f32)[:, None],
        upstream[0],
        w_wide,
        x_first,
        w_shrink,
        y_first,
    )
    embedded, grad_resid_one, first, active, second, plow, two, lifted, one, sums = results[:10]
    grads = [send(g, r) for r, g in enumerate(results[10:])]

    slabs = hidden // width
    backs = []
    landed = []
    inputs = (joined, grads, mixed_own, stats)

    def backward(h, inputs):
        back = attend_backward(*inputs, h)
        backs.append(back)
        landed.append([send(back[r], -r) for r in range(parts)])

    if fast:
        first, rest = together(first, rest)
        w_rest = [rest, swap(rest, 4)]
        keep, give = weight_grads(
            turn, where, arrived, first, active, second, plow, two, lifted, one, sums, dp
        )
        grads, give, w_rest = together(grads, give, w_rest)
        other = swap(give, 1)
        w_rest += [swap(w, 1) for w in w_rest]
        inputs, keep = together((joined, grads, mixed_own, stats), keep)
        backward(0, inputs)
        keep, other, backs[0] = together(keep, other, backs[0])
        batch = sum_dp_core(keep, other)
        inputs, batch, w_rest = together(inputs, batch, w_rest)
        batch = sum_dp_first(batch)
        backward(1, inputs)
        inputs, landed[0], backs[1] = together(inputs, landed[0], backs[1])
        backward(2, inputs)
        batch, landed[1], backs = together(batch, landed[1], backs)
        batch = sum_dp_second(batch)
        backs, batch = together(backs, batch)
        batch = sum_dp_last(batch)
        keep, give = triple_grads(turn, blocks, backs, dp)
        give, batch, landed[2] = together(give, batch, landed[2])
        halves = [add(batch[0], batch[1]), add(batch[2], batch[3])]
        halves = [sum_seq_first(v) for v in halves]
        last = add(keep, swap(give, 1))
        last = add(last[:2], swap(last[2:], 2))
        last = add(last[0], swap(last[1], 4))
        halves = [sum_seq_second(v) for v in halves]
        halves[1], last = together(halves[1], last)
        last = [last, swap_seq(last, 2)]
        pairs = [jnp.stack([v, swap_seq(v, 2)]) for v in halves]
        pairs[0], last = together(pairs[0], last)
        last += [swap_seq(v, 1) for v in last]
        r_triple, r_queries, r_values = unpack_triple(where, turn, last, heads)
        pairs = [v for pair in pairs for v in (pair, swap_seq(pair, 1))]
        input_grad = input_gradient(turn, grad_resid_one, w_own, landed, w_rest, x_first)
        pairs, r_triple, input_grad = together(pairs, r_triple, input_grad)
        outs = unpack(where, turn, pairs, dp, hidden, emb)
        r_shrink, r_expand, r_mixer, r_project = outs[:4]
        r_offset, r_gamma, r_beta, r_settle, r_gain, r_shift, r_lift = outs[4:]
    else:
        g_expand = dot(first, lifted, TN).astype(bf16)
        mixed = jnp.concatenate(arrived, axis=1)
        g_mixer = jnp.roll(dot(mixed, one, TN).reshape(parts, local, width), place, axis=0)
        g_project = dot(second, plow, TN).astype(bf16)
        batch = jnp.concatenate(
            [
                dot(active, two, TN).astype(bf16).reshape(dp, hlines, width),
                *[
                    g_expand[:, c * width : (c + 1) * width].reshape(dp, lines, width)
                    for c in range(slabs)
                ],
                g_mixer.astype(bf16).reshape(dp, lines, width),
                jnp.stack([rows_of([g[None].reshape(1, -1)], 1, width)[0] for g in g_project.reshape(dp, lines, emb)]),
                jnp.broadcast_to(sums.astype(bf16), (dp,) + sums.shape),
            ],
            axis=1,
        )
        batch = lax.psum_scatter(batch, "dp", scatter_dimension=0, tiled=False)
        batch = lax.psum(batch, "seq")
        for h in range(heads):
            backward(h, inputs)
        g_own = jnp.concatenate([jnp.concatenate(back, axis=0) for back in backs], axis=1)
        g_triple = dot(jnp.concatenate(blocks, axis=0), g_own, TN)
        columns = jnp.sum(g_own.astype(f32), axis=0).astype(bf16)
        last = jnp.concatenate(
            [
                g_triple.astype(bf16).reshape(dp, lines, 3 * local),
                jnp.broadcast_to(columns, (dp, 1, 3 * local)),
            ],
            axis=1,
        )
        last = lax.psum_scatter(last, "dp", scatter_dimension=0, tiled=False)
        last = lax.all_gather(last, "seq", axis=0, tiled=False)
        batch = batch.astype(f32)
        r_shrink = batch[:hlines]
        at = hlines
        r_expand = jnp.concatenate(
            [batch[at + c * lines : at + (c + 1) * lines] for c in range(slabs)], axis=1
        )
        at += lines * slabs
        r_mixer = batch[at : at + lines]
        at += lines
        piece = lines * emb // width
        r_project = batch[at : at + piece].reshape(lines, emb)
        tail = batch[at + piece :]
        r_offset, r_gamma, r_beta, r_settle, r_gain, r_shift = [
            lax.dynamic_slice(tail[i], (mine * lines,), (lines,)) for i in range(6)
        ]
        r_lift = lax.dynamic_slice(
            tail[6 : 6 + slabs].reshape(hidden), (mine * hlines,), (hlines,)
        )

        last = last.astype(f32)
        last = last.reshape(parts, lines + 1, heads, 3, HD).transpose(1, 3, 0, 2, 4)
        r_triple = last[:lines].reshape(lines, 3 * width)
        sums = last[lines].reshape(3, width)
        r_queries = lax.dynamic_slice(sums[0], (mine * lines,), (lines,))
        r_values = lax.dynamic_slice(sums[2], (mine * lines,), (lines,))
        input_grad = input_gradient(turn, grad_resid_one, w_own, landed, w_rest, x_first)
    return (
        embedded[None],
        input_grad[None],
        r_triple,
        r_queries,
        r_values,
        r_mixer,
        r_offset,
        r_gamma,
        r_beta,
        r_expand,
        r_lift,
        r_shrink,
        r_settle,
        r_gain,
        r_shift,
        r_project,
    )


def solution(mesh):
    whole = P("dp", "seq", None)
    rows = P("dp", None)
    flat = P("dp")
    in_specs = (
        whole,
        rows,
        flat,
        flat,
        rows,
        flat,
        flat,
        flat,
        rows,
        flat,
        rows,
        flat,
        flat,
        flat,
        rows,
        P("dp", "seq"),
        whole,
    )
    out_specs = (
        whole,
        whole,
        rows,
        flat,
        flat,
        rows,
        flat,
        flat,
        flat,
        rows,
        flat,
        rows,
        flat,
        flat,
        flat,
        rows,
    )
    return jax.shard_map(shards, mesh=mesh, in_specs=in_specs, out_specs=out_specs, check_vma=False)
```
